512 devices in a mesh: row: 16 (over z, core), col: 32 (over y, x).
Axes of the slice: x: 4, y: 8, z: 8, core: 2. Of those that a mesh axis runs over, the one named last changes fastest.
Arguments:
- pivots: int32 [2], replicated, may hold values from 0 to 63, as said below
- demand: float32 [16384, 512], P('row', 'col'), may hold values from -0.09 to 0.09
- prices: float32 [512, 16384], P('row', 'col'), may hold values from -0.09 to 0.09
Outputs:
- reduced: float32 [16384, 16384], P('row', 'col')
The draws below stay inside these ranges and needn't reach their ends.
Inputs may be any that keep to these rules, and one draw needn't show every extreme that they name: `pivots`: two different panel indices, one of which is the last panel.
All inputs are finite; a program needn't handle non-finite values.
Results may differ from the reference program's by a relative error of at most 0.0003.
Values sent between devices are 32-bit elements; how exact they have to be, the bound alone decides.
No kernel may reach another device: no remote copies, remote signals or barrier semaphores. Data moves between devices by JAX's collectives and lax.ppermute only.
A program may use at most 64 MiB of HBM per device.

```python
import jax
import jax.numpy as jnp
from jax import lax

K = 512
PW = 256
N = 16384


def slab_values(key, shape):
    return jnp.clip(0.007 + 0.03 * jax.random.normal(key, shape, jnp.float32), -0.09, 0.09)


def draw_pivots(key, part):
    panels = N // PW
    last_panel = jnp.int32(panels - 1)
    other = jax.random.randint(jax.random.fold_in(key, 7), (), 0, panels - 1).astype(jnp.int32)
    flipped = jax.random.randint(jax.random.fold_in(key, 19), (), 0, 2)
    leading = jnp.where(flipped == 1, last_panel, other)
    trailing = jnp.where(flipped == 1, other, last_panel)
    return jnp.stack([leading, trailing]).astype(jnp.int32)


def draw_demand(key, part):
    return slab_values(jax.random.fold_in(key, 11), (N, K))


def draw_prices(key, part):
    return slab_values(jax.random.fold_in(key, 13), (K, N))


def setup_inputs(seed: int = 0) -> dict:
    keys = jax.random.split(jax.random.key(seed), 4)
    pivots = draw_pivots(jax.random.fold_in(keys[3], 71), 0)
    demand = draw_demand(jax.random.fold_in(keys[3], 71), 0)
    prices = draw_prices(jax.random.fold_in(keys[3], 71), 0)
    return dict(pivots=pivots, demand=demand, prices=prices)


def product(left, right):
    return jnp.dot(left.astype(jnp.float32), right.astype(jnp.float32), precision=lax.Precision.HIGHEST, preferred_element_type=jnp.float32)

def reference(pivots, demand, prices):
    matrix = jnp.eye(N, dtype=jnp.float32) - product(demand, prices)
    for which in range(2):
        first = (pivots[which] * PW).astype(jnp.int32)
        pivot_block = lax.dynamic_slice(matrix, (first, first), (PW, PW))
        row_panel = lax.dynamic_slice_in_dim(matrix, first, PW, 0)
        column_panel = lax.dynamic_slice_in_dim(matrix, first, PW, 1)
        solved = jnp.linalg.solve(pivot_block, row_panel)
        matrix = matrix - product(column_panel, solved)
    return matrix
```

```python
import functools

import jax
import jax.numpy as jnp
from jax import lax
from jax.experimental import pallas as pl
from jax.experimental.pallas import tpu as pltpu
from jax.sharding import Mesh
from jax.sharding import PartitionSpec as P

PW = 256
K = 512
NZ, NCORE, NY, NX = 8, 2, 8, 4
ROW = ("z", "core")
COL = ("y", "x")


def ring(n, step):
    return [(i, (i + step) % n) for i in range(n)]


def flip(n, bit):
    return [(i, i ^ bit) for i in range(n)]


def spread(panels, roots, hops):
    half = panels.shape[1] // 2
    first = lax.broadcasted_iota(jnp.int32, (1, panels.shape[1]), 1) < half
    done = {}
    for axis, n, bit in hops:
        got = lax.ppermute(panels, axis, flip(n, bit))
        takes = []
        for root in roots:
            same = True
            for other, size in (("z", NZ), ("core", NCORE), ("y", NY), ("x", NX)):
                if other not in root:
                    continue
                me = lax.axis_index(other)
                if other == axis:
                    me = me ^ bit
                left = (size - 1) & ~done.get(other, 0)
                same = same & ((me & left) == (root[other] & left))
            takes.append(same)
        panels = jnp.where(jnp.where(first, takes[0], takes[1]), got, panels)
        done[axis] = done.get(axis, 0) | bit
    return panels


def split(a):
    high = a.astype(jnp.bfloat16)
    return high, (a - high.astype(jnp.float32)).astype(jnp.bfloat16)


def dot1(a, b):
    return jnp.dot(a, b, preferred_element_type=jnp.float32)


def dot3(a, b):
    return dot1(a[0], b[0]) + (dot1(a[0], b[1]) + dot1(a[1], b[0]))


def eye(rows, cols):
    r = lax.broadcasted_iota(jnp.int32, (rows, cols), 0)
    c = lax.broadcasted_iota(jnp.int32, (rows, cols), 1)
    return (r == c).astype(jnp.float32)


def solve_kernel(
    at, own, other, d0, d1, d2, d3a, d3b, v_ref, pj, pc, dj, x_ref, bh_ref, bl_ref, r_ref
):
    z, core, y, x, first, second = (at[i] for i in range(6))
    for k in range(NZ):
        source = (z + (k + 5)) & 7
        for ref, side in ((own, core), (other, 1 - core)):
            to = pl.ds(pl.multiple_of((2 * source + side) * 32, 32), 32)
            pc[to, :] = ref[pl.ds(32 * k, 32), :K]
            pj[to, :] = ref[pl.ds(32 * k, 32), K:]
    for p in range(NY):
        source = 4 * (y ^ ((p & 1) * 4 + (p & 2) + p // 4))
        for ref, step in ((d0, 0), (d1, 3), (d2, 1), (None, 2)):
            to = pl.ds(pl.multiple_of((source + ((x + step) & 3)) * 16, 16), 16)
            if ref is None:
                if p < 4:
                    dj[to, :] = d3a[pl.ds(16 * p, 16), :]
                else:
                    dj[to, :] = d3b[pl.ds(16 * (p - 4), 16), :]
            else:
                dj[to, :] = ref[pl.ds(16 * p, 16), :]
    b = eye(K, K) - lax.dot_general(
        pj[...], dj[...], (((1,), (1,)), ((), ())),
        precision=lax.Precision.HIGHEST, preferred_element_type=jnp.float32,
    )
    r_ref[...] = b
    size = jnp.max(jnp.sum(jnp.abs(b), axis=0)) * jnp.max(jnp.sum(jnp.abs(b), axis=1))
    bh, bl = split(b)
    bh_ref[...] = bh
    bl_ref[...] = bl
    start = b.T / size
    x_ref[...] = start

    def coarse(carry):
        count, _ = carry
        xv = x_ref[...]
        xh = xv.astype(jnp.bfloat16)
        r = eye(K, K) - dot1(bh_ref[...], xh)
        x_ref[...] = xv + dot1(xh, r.astype(jnp.bfloat16))
        return count + 1, jnp.sum(r * r)

    lax.while_loop(
        lambda c: (c[0] < 40) & (c[1] > 0.3) & (c[1] < 4.0 * K),
        coarse,
        (jnp.int32(0), jnp.float32(K)),
    )

    def residual(xv):
        return eye(K, K) - dot3((bh_ref[...], bl_ref[...]), split(xv))

    left = residual(x_ref[...])

    @pl.when(jnp.logical_not(jnp.sum(left * left) < 1.0 * K))
    def _():
        x_ref[...] = r_ref[...].T / size

    def fine(carry):
        count, last, _ = carry
        xv = x_ref[...]
        r = residual(xv)
        x_ref[...] = xv + dot3(split(xv), split(r))
        now = jnp.sum(r * r)
        stuck = (now > 0.25 * last) & (now < 0.1)
        return count + 1, now, (now > 3e-3) & jnp.logical_not(stuck)

    lax.while_loop(
        lambda c: (c[0] < 60) & c[2],
        fine,
        (jnp.int32(0), jnp.float32(2.0 * K), jnp.bool_(True)),
    )
    xv = x_ref[...]
    r = eye(K, K) - jnp.dot(
        r_ref[...], xv, precision=lax.Precision.HIGHEST, preferred_element_type=jnp.float32
    )
    xv = xv + dot3(split(xv), split(r))
    v = dot3(split(xv), split(pc[...]))
    col = lax.broadcasted_iota(jnp.int32, (1, K), 1) + (y * NX + x) * K
    gone = (col // PW == first) | (col // PW == second)
    v_ref[...] = jnp.where(gone, 0.0, v)


def solve(at, *parts):
    f32 = jnp.float32
    return pl.pallas_call(
        solve_kernel,
        out_shape=jax.ShapeDtypeStruct((K, K), f32),
        in_specs=[pl.BlockSpec(memory_space=pltpu.SMEM)]
        + [pl.BlockSpec(memory_space=pltpu.VMEM)] * len(parts),
        out_specs=pl.BlockSpec(memory_space=pltpu.VMEM),
        scratch_shapes=[pltpu.VMEM((K, K), f32)] * 4
        + [pltpu.VMEM((K, K), jnp.bfloat16)] * 2
        + [pltpu.VMEM((K, K), f32)],
        cost_estimate=pl.CostEstimate(
            flops=60 * 2 * K**3, bytes_accessed=5 << 20, transcendentals=0
        ),
    )(at, *parts)


def on_device(pivots, demand, prices):
    z, core, y, x = (lax.axis_index(name) for name in ("z", "core", "y", "x"))
    demand_rows = lax.all_gather(demand, COL, axis=1, tiled=True)
    row_roots, col_roots, demand_parts, price_parts = [], [], [], []
    for which in range(2):
        pivot = pivots[which]
        row, col = pivot // 4, pivot // 2
        row_roots.append({"z": row // 2, "core": row % 2})
        col_roots.append({"y": col // 4, "x": col % 4})
        demand_parts.append(lax.dynamic_slice_in_dim(demand, (pivot % 4) * PW, PW, 0).T)
        price_parts.append(lax.dynamic_slice_in_dim(prices, (pivot % 2) * PW, PW, 1))
    price_panels = spread(
        jnp.concatenate(price_parts, 1), col_roots,
        (("y", NY, 4), ("y", NY, 2), ("y", NY, 1), ("x", NX, 2), ("x", NX, 1)),
    )
    demand_panels = spread(
        jnp.concatenate(demand_parts, 1), row_roots,
        (("z", NZ, 4), ("z", NZ, 2), ("z", NZ, 1), ("core", NCORE, 1)),
    )
    block = jnp.concatenate([prices, price_panels], 1)
    below, above = [block], [block]
    for step in range(4):
        below.append(lax.ppermute(below[-1], "z", ring(NZ, 1)))
        if step < 3:
            above.append(lax.ppermute(above[-1], "z", ring(NZ, -1)))
    own = jnp.concatenate(below[3:0:-1] + above + below[4:], 0)
    other = lax.ppermute(own, "core", flip(NCORE, 1))
    held = demand_panels
    for bit in (4, 2, 1):
        held = jnp.concatenate([held, lax.ppermute(held, "y", flip(NY, bit))], 0)
    left = lax.ppermute(held, "x", ring(NX, 1))
    right = lax.ppermute(held, "x", ring(NX, -1))
    far_a = lax.ppermute(left[: 64], "x", ring(NX, 1))
    far_b = lax.ppermute(right[64:], "x", ring(NX, -1))
    at = jnp.stack([z, core, y, x, pivots[0], pivots[1]]).astype(jnp.int32)
    v = solve(at, own, other, held, left, right, far_a, far_b)
    rows = (z * NCORE + core) * demand_rows.shape[0] + jnp.arange(demand_rows.shape[0])
    cols = (y * NX + x) * K + jnp.arange(K)
    kept = (rows // PW != pivots[0]) & (rows // PW != pivots[1])
    identity = (rows[:, None] == cols[None, :]).astype(jnp.float32)
    tile = identity - jnp.dot(
        demand_rows, v, precision=lax.Precision.HIGH, preferred_element_type=jnp.float32
    )
    return jnp.where(kept[:, None], tile, 0.0)


def solution(mesh):
    inner = Mesh(mesh.devices.reshape(NZ, NCORE, NY, NX), ROW + COL)
    placed = (P(), P(ROW, COL), P(ROW, COL))
    return jax.shard_map(
        on_device, mesh=inner, in_specs=placed, out_specs=P(ROW, COL), check_vma=False
    )
```

```python
import jax
import jax.numpy as jnp
from jax import lax
from jax.experimental import pallas as pl
from jax.experimental.pallas import tpu as pltpu
from jax.sharding import Mesh
from jax.sharding import PartitionSpec as P

PW = 256
K = 512
NZ, NCORE, NY, NX = 8, 2, 8, 4
ROW = ("z", "core")
COL = ("y", "x")


def flip(n, bit):
    return [(i, i ^ bit) for i in range(n)]


class Spread:
    def __init__(self, panels, roots):
        self.panels, self.roots, self.done = panels, roots, {}

    def hop(self, axis, n, bit):
        got = lax.ppermute(self.panels, axis, flip(n, bit))
        takes = []
        for root in self.roots:
            same = True
            for other, target in root.items():
                me = lax.axis_index(other)
                if other == axis:
                    me = me ^ bit
                left = 7 & ~self.done.get(other, 0)
                same = same & ((me & left) == (target & left))
            takes.append(same)
        width = self.panels.shape[1]
        first = lax.broadcasted_iota(jnp.int32, (1, width), 1) < width // 2
        take = (first & takes[0]) | (jnp.logical_not(first) & takes[1])
        self.panels = jnp.where(take, got, self.panels)
        self.done[axis] = self.done.get(axis, 0) | bit


def split(a):
    high = a.astype(jnp.bfloat16)
    return high, (a - high.astype(jnp.float32)).astype(jnp.bfloat16)


def dot1(a, b):
    return jnp.dot(a, b, preferred_element_type=jnp.float32)


def dot3(a, b):
    return dot1(a[0], b[0]) + (dot1(a[0], b[1]) + dot1(a[1], b[0]))


def eye(rows, cols):
    r = lax.broadcasted_iota(jnp.int32, (rows, cols), 0)
    c = lax.broadcasted_iota(jnp.int32, (rows, cols), 1)
    return (r == c).astype(jnp.float32)


def pack_kernel(at, p_ref, d_ref, g_ref):
    s = (4 * at[2] + at[3]) & 7
    block = lax.dot_general(
        p_ref[...], jnp.concatenate([d_ref[...]] * 8, 0), (((1,), (1,)), ((), ())),
        precision=lax.Precision.HIGHEST, preferred_element_type=jnp.float32,
    )
    b = lax.broadcasted_iota(jnp.int32, (8, 128), 0)
    group = lax.broadcasted_iota(jnp.int32, (8, 128), 1) // 16
    kept = group == ((b + s) & 7)
    row = lax.broadcasted_iota(jnp.int32, (4, 128), 0)
    packed = jnp.zeros((4, 128), jnp.float32)
    for a in range(4):
        line = jnp.sum(jnp.where(kept, block[8 * a : 8 * a + 8], 0.0), axis=0, keepdims=True)
        packed = jnp.where(row == a, line, packed)
    for k in range(NZ):
        g_ref[k] = packed


def pack(at, p, d):
    return pl.pallas_call(
        pack_kernel,
        out_shape=jax.ShapeDtypeStruct((NZ, 4, 128), jnp.float32),
        in_specs=[pl.BlockSpec(memory_space=pltpu.SMEM)]
        + [pl.BlockSpec(memory_space=pltpu.VMEM)] * 2,
        out_specs=pl.BlockSpec(memory_space=pltpu.VMEM),
    )(at, p, d)


def row_order(shape):
    r = lax.broadcasted_iota(jnp.int32, shape, 0)
    return ((r >> 2) & 7) * 64 + ((r >> 5) & 1) * 32 + (r & 3) * 8 + (r >> 6)


def invert_kernel(at, own, other, w_ref, x_ref, b_ref, bh_ref, bl_ref):
    core = at[1]
    group = lax.broadcasted_iota(jnp.int32, (32, 128), 1) // 16
    for ref, side in ((own, core), (other, 1 - core)):
        for q in range(4):
            pieces = [
                ref[pl.ds(((s % 4) * 8 + 2 * q + s // 4) * 32, 32), :] for s in range(8)
            ]
            for b in range(8):
                line = pieces[0]
                for s in range(1, 8):
                    line = jnp.where(group == (b + s) % 8, pieces[s], line)
                if b:
                    line = pltpu.roll(line, 128 - 16 * b, 1)
                to = pl.ds(pl.multiple_of(b * 64 + side * 32, 32), 32)
                b_ref[to, 128 * q : 128 * q + 128] = line
    unit = (
        row_order((K, K)) == lax.broadcasted_iota(jnp.int32, (K, K), 1)
    ).astype(jnp.float32)
    b = unit - b_ref[...]
    b_ref[...] = b
    size = jnp.max(jnp.sum(jnp.abs(b), axis=0)) * jnp.max(jnp.sum(jnp.abs(b), axis=1))
    bh, bl = split(b)
    bh_ref[...] = bh
    bl_ref[...] = bl
    x_ref[...] = b.T / size

    def coarse(carry):
        count, _ = carry
        xv = x_ref[...]
        xh = xv.astype(jnp.bfloat16)
        r = eye(K, K) - dot1(bh_ref[...], xh)
        x_ref[...] = xv + dot1(xh, r.astype(jnp.bfloat16))
        return count + 1, jnp.sum(r * r)

    lax.while_loop(
        lambda c: (c[0] < 40) & (c[1] > 0.3) & (c[1] < 4.0 * K),
        coarse,
        (jnp.int32(0), jnp.float32(K)),
    )

    def residual(xv):
        return eye(K, K) - dot3((bh_ref[...], bl_ref[...]), split(xv))

    left = residual(x_ref[...])

    @pl.when(jnp.logical_not(jnp.sum(left * left) < 1.0 * K))
    def _():
        x_ref[...] = b_ref[...].T / size

    def fine(carry):
        count, last, _ = carry
        xv = x_ref[...]
        r = residual(xv)
        x_ref[...] = xv + dot3(split(xv), split(r))
        now = jnp.sum(r * r)
        stuck = (now > 0.25 * last) & (now < 0.1)
        return count + 1, now, (now > 3e-3) & jnp.logical_not(stuck)

    lax.while_loop(
        lambda c: (c[0] < 60) & c[2],
        fine,
        (jnp.int32(0), jnp.float32(2.0 * K), jnp.bool_(True)),
    )
    xv = x_ref[...]
    r = eye(K, K) - jnp.dot(
        b_ref[...], xv, precision=lax.Precision.HIGHEST, preferred_element_type=jnp.float32
    )
    high, low = split(xv + dot3(split(xv), split(r)))
    order = unit.astype(jnp.bfloat16)
    w_ref[...] = dot1(high, order) + dot1(low, order)


def invert(at, own, other):
    f32 = jnp.float32
    return pl.pallas_call(
        invert_kernel,
        out_shape=jax.ShapeDtypeStruct((K, K), f32),
        in_specs=[pl.BlockSpec(memory_space=pltpu.SMEM)]
        + [pl.BlockSpec(memory_space=pltpu.VMEM)] * 2,
        out_specs=pl.BlockSpec(memory_space=pltpu.VMEM),
        scratch_shapes=[pltpu.VMEM((K, K), f32)] * 2 + [pltpu.VMEM((K, K), jnp.bfloat16)] * 2,
        cost_estimate=pl.CostEstimate(
            flops=60 * 2 * K**3, bytes_accessed=5 << 20, transcendentals=0
        ),
    )(at, own, other)


STEP = 256


def tile_kernel(at, w_ref, p_ref, d_ref, o_ref, vh_ref, vl_ref):
    z, core, y, x, first, second = (at[i] for i in range(6))
    step = pl.program_id(0)
    col = lax.broadcasted_iota(jnp.int32, (1, K), 1) + (y * NX + x) * K

    @pl.when(step == 0)
    def _():
        v = dot3(split(w_ref[...]), split(p_ref[...]))
        gone = (col // PW == first) | (col // PW == second)
        vh, vl = split(jnp.where(gone, 0.0, v))
        vh_ref[...] = vh
        vl_ref[...] = vl

    base = (z * NCORE + core) * 1024 + step * STEP
    d = split(d_ref[...].T)
    row = lax.broadcasted_iota(jnp.int32, (STEP, 1), 0) + base
    kept = (base // PW != first) & (base // PW != second)
    tile = (row == col).astype(jnp.float32) - dot3(d, (vh_ref[...], vl_ref[...]))
    o_ref[...] = jnp.where(kept, tile, 0.0)


def tile(at, w, p, d):
    f32, bf16 = jnp.float32, jnp.bfloat16
    rows = d.shape[1]
    return pl.pallas_call(
        tile_kernel,
        grid=(rows // STEP,),
        out_shape=jax.ShapeDtypeStruct((rows, K), f32),
        in_specs=[
            pl.BlockSpec(memory_space=pltpu.SMEM),
            pl.BlockSpec((K, K), lambda i: (0, 0)),
            pl.BlockSpec((K, K), lambda i: (0, 0)),
            pl.BlockSpec((K, STEP), lambda i: (0, i)),
        ],
        out_specs=pl.BlockSpec((STEP, K), lambda i: (i, 0)),
        scratch_shapes=[pltpu.VMEM((K, K), bf16)] * 2,
        cost_estimate=pl.CostEstimate(
            flops=9 * 2 * K**3, bytes_accessed=6 << 20, transcendentals=0
        ),
    )(at, w, p, d)


def gather(block, axis, n):
    out = lax.all_to_all(jnp.broadcast_to(block[None], (n,) + block.shape), axis, 0, 0)
    return out.reshape((-1,) + block.shape[1:])


def on_device(pivots, demand, prices):
    z, core, y, x = (lax.axis_index(name) for name in ("z", "core", "y", "x"))
    at = jnp.stack([z, core, y, x, pivots[0], pivots[1]]).astype(jnp.int32)
    flat = demand.T
    demand_all = lax.all_gather(gather(flat, "x", NX), "y", axis=0, tiled=True)
    twin = lax.ppermute(prices, "core", flip(NCORE, 1))
    pair = jnp.concatenate(
        [jnp.where(core == 0, prices, twin), jnp.where(core == 0, twin, prices)], 0
    )
    prices_all = lax.all_gather(pair, "z", axis=0, tiled=True)
    row_roots, col_roots, demand_parts, price_parts = [], [], [], []
    for which in range(2):
        pivot = pivots[which]
        row, col = pivot // 4, pivot // 2
        row_roots.append({"z": row // 2, "core": row % 2})
        col_roots.append({"y": col // 4, "x": col % 4})
        demand_parts.append(lax.dynamic_slice_in_dim(flat, (pivot % 4) * PW, PW, 1))
        price_parts.append(lax.dynamic_slice_in_dim(prices, (pivot % 2) * PW, PW, 1))
    p = Spread(jnp.concatenate(price_parts, 1), col_roots)
    d = Spread(jnp.concatenate(demand_parts, 1), row_roots)
    for hop, other_hop in (
        (("y", NY, 4), ("z", NZ, 4)),
        (("y", NY, 2), ("z", NZ, 2)),
        (("y", NY, 1), ("z", NZ, 1)),
        (("x", NX, 2), ("core", NCORE, 1)),
        (("x", NX, 1), None),
    ):
        p.panels, d.panels = lax.optimization_barrier((p.panels, d.panels))
        p.hop(*hop)
        if other_hop:
            d.hop(*other_hop)
    packed = lax.all_to_all(pack(at, p.panels, d.panels), "z", 0, 0).reshape(NZ * 4, 128)
    packed = gather(gather(packed, "y", NY), "x", NX)
    w = invert(at, packed, lax.ppermute(packed, "core", flip(NCORE, 1)))
    return tile(at, w, prices_all, demand_all)


def solution(mesh):
    inner = Mesh(mesh.devices.reshape(NZ, NCORE, NY, NX), ROW + COL)
    placed = (P(), P(ROW, COL), P(ROW, COL))
    return jax.shard_map(
        on_device, mesh=inner, in_specs=placed, out_specs=P(ROW, COL), check_vma=False
    )
```

```python
import jax
import jax.numpy as jnp
from jax import lax
from jax.experimental import pallas as pl
from jax.experimental.pallas import tpu as pltpu
from jax.sharding import Mesh
from jax.sharding import PartitionSpec as P

PW = 256
K = 512
FAST, GAIN = 5, 1.7
NZ, NCORE, NY, NX = 8, 2, 8, 4
ROW = ("z", "core")
COL = ("y", "x")


def flip(n, bit):
    return [(i, i ^ bit) for i in range(n)]


def split(a):
    high = a.astype(jnp.bfloat16)
    return high, (a - high.astype(jnp.float32)).astype(jnp.bfloat16)


def dot1(a, b):
    return jnp.dot(a, b, preferred_element_type=jnp.float32)


def dot3(a, b):
    return dot1(a[0], b[0]) + (dot1(a[0], b[1]) + dot1(a[1], b[0]))


def eye(rows, cols):
    r = lax.broadcasted_iota(jnp.int32, (rows, cols), 0)
    c = lax.broadcasted_iota(jnp.int32, (rows, cols), 1)
    return (r == c).astype(jnp.float32)


def cut_kernel(at, p_ref, d_ref, pp_ref, dp_ref):
    for q in range(4):
        pivot = at[4 + q // 2]
        start = pl.multiple_of((pivot & 1) * PW + (q % 2) * 128, 128)
        pp_ref[pl.ds(q, 32, stride=4), :] = p_ref[:, pl.ds(start, 128)]
        start = pl.multiple_of((pivot & 3) * PW + (q % 2) * 128, 128)
        dp_ref[pl.ds(q, 16, stride=4), :] = d_ref[:, pl.ds(start, 128)]


def pick_kernel(at, p_ref, d_ref, o_ref):
    row = lax.broadcasted_iota(jnp.int32, (8, 128), 0)
    packed = jnp.zeros((8, 128), jnp.float32)
    for q in range(4):
        pivot = at[4 + q // 2]
        packed = jnp.where(row == q, p_ref[pl.ds(4 * (pivot // 2) + q, 1), :], packed)
        packed = jnp.where(row == 4 + q, d_ref[pl.ds(4 * (pivot // 4) + q, 1), :], packed)
    for k in range(NZ):
        o_ref[pl.ds(8 * k, 8), :] = packed


def small(kernel, shapes, at, *parts):
    return pl.pallas_call(
        kernel,
        out_shape=[jax.ShapeDtypeStruct(shape, jnp.float32) for shape in shapes],
        in_specs=[pl.BlockSpec(memory_space=pltpu.SMEM)]
        + [pl.BlockSpec(memory_space=pltpu.VMEM)] * len(parts),
        out_specs=[pl.BlockSpec(memory_space=pltpu.VMEM)] * len(shapes),
    )(at, *parts)


def slab_row(n, of_prices):
    row = 2 * (n & 7) + (n >> 8)
    col = 4 * ((n >> 3) & 7) + ((n >> 6) & 3)
    return 32 * row + col if of_prices else 16 * col + row


def invert_kernel(at, own, other, w_ref, x_ref, b_ref, bh_ref, bl_ref, pj_ref, dj_ref):
    core = at[1]
    for ref, side in ((own, core), (other, 1 - core)):
        to = pl.ds(pl.multiple_of(side * 256, 256), 256)
        for q in range(4):
            pj_ref[to, 128 * q : 128 * q + 128] = ref[pl.ds(q, 256, stride=8), :]
            dj_ref[to, 128 * q : 128 * q + 128] = ref[pl.ds(q + 4, 256, stride=8), :]
    n0 = lax.broadcasted_iota(jnp.int32, (K, K), 0)
    n1 = lax.broadcasted_iota(jnp.int32, (K, K), 1)
    unit = (slab_row(n0, True) == slab_row(n1, False)).astype(jnp.float32)
    b = unit - lax.dot_general(
        pj_ref[...], dj_ref[...], (((1,), (1,)), ((), ())),
        precision=lax.Precision.HIGHEST, preferred_element_type=jnp.float32,
    )
    b_ref[...] = b
    size = jnp.max(jnp.sum(jnp.abs(b), axis=0)) * jnp.max(jnp.sum(jnp.abs(b), axis=1))
    bh, bl = split(b)
    bh_ref[...] = bh
    bl_ref[...] = bl
    x_ref[...] = b.T / size

    def coarse(carry):
        count, _ = carry
        xv = x_ref[...]
        xh = xv.astype(jnp.bfloat16)
        r = eye(K, K) - dot1(bh_ref[...], xh)
        gain = jnp.where(count < FAST, GAIN, 1.0)
        x_ref[...] = gain * (xv + dot1(xh, r.astype(jnp.bfloat16)))
        return count + 1, jnp.sum(r * r)

    lax.while_loop(
        lambda c: (c[0] < 40) & (c[1] > 0.3) & (c[1] < 4.0 * K),
        coarse,
        (jnp.int32(0), jnp.float32(K)),
    )

    def residual(xv):
        return eye(K, K) - dot3((bh_ref[...], bl_ref[...]), split(xv))

    left = residual(x_ref[...])

    @pl.when(jnp.logical_not(jnp.sum(left * left) < 1.0 * K))
    def _():
        x_ref[...] = b_ref[...].T / size

    def fine(carry):
        count, last, _ = carry
        xv = x_ref[...]
        r = residual(xv)
        x_ref[...] = xv + dot3(split(xv), split(r))
        now = jnp.sum(r * r)
        stuck = (now > 0.25 * last) & (now < 0.1)
        return count + 1, now, (now > 3e-3) & jnp.logical_not(stuck)

    lax.while_loop(
        lambda c: (c[0] < 60) & c[2],
        fine,
        (jnp.int32(0), jnp.float32(2.0 * K), jnp.bool_(True)),
    )
    xv = x_ref[...]
    r = eye(K, K) - jnp.dot(
        b_ref[...], xv, precision=lax.Precision.HIGHEST, preferred_element_type=jnp.float32
    )
    high, low = split(xv + dot3(split(xv), split(r)))
    left = (n0 == slab_row(n1, False)).astype(jnp.bfloat16)
    right = (slab_row(n0, True) == n1).astype(jnp.bfloat16)
    high = dot1(high, right).astype(jnp.bfloat16)
    low = dot1(low, right).astype(jnp.bfloat16)
    w_ref[...] = dot1(left, high) + dot1(left, low)


def invert(at, own, other):
    f32 = jnp.float32
    return pl.pallas_call(
        invert_kernel,
        out_shape=jax.ShapeDtypeStruct((K, K), f32),
        in_specs=[pl.BlockSpec(memory_space=pltpu.SMEM)]
        + [pl.BlockSpec(memory_space=pltpu.VMEM)] * 2,
        out_specs=pl.BlockSpec(memory_space=pltpu.VMEM),
        scratch_shapes=[pltpu.VMEM((K, K), f32)] * 2
        + [pltpu.VMEM((K, K), jnp.bfloat16)] * 2
        + [pltpu.VMEM((K, K), f32)] * 2,
        cost_estimate=pl.CostEstimate(
            flops=60 * 2 * K**3, bytes_accessed=5 << 20, transcendentals=0
        ),
    )(at, own, other)


STEP = 256


def tile_kernel(at, w_ref, p_ref, d_ref, o_ref, vh_ref, vl_ref):
    z, core, y, x, first, second = (at[i] for i in range(6))
    step = pl.program_id(0)
    col = lax.broadcasted_iota(jnp.int32, (1, K), 1) + (y * NX + x) * K

    @pl.when(step == 0)
    def _():
        v = dot3(split(w_ref[...]), split(p_ref[...]))
        gone = (col // PW == first) | (col // PW == second)
        vh, vl = split(jnp.where(gone, 0.0, v))
        vh_ref[...] = vh
        vl_ref[...] = vl

    base = (z * NCORE + core) * 1024 + step * STEP
    d = split(d_ref[...].T)
    row = lax.broadcasted_iota(jnp.int32, (STEP, 1), 0) + base
    kept = (base // PW != first) & (base // PW != second)
    tile = (row == col).astype(jnp.float32) - dot3(d, (vh_ref[...], vl_ref[...]))
    o_ref[...] = jnp.where(kept, tile, 0.0)


def tile(at, w, p, d):
    f32, bf16 = jnp.float32, jnp.bfloat16
    rows = d.shape[1]
    return pl.pallas_call(
        tile_kernel,
        grid=(rows // STEP,),
        out_shape=jax.ShapeDtypeStruct((rows, K), f32),
        in_specs=[
            pl.BlockSpec(memory_space=pltpu.SMEM),
            pl.BlockSpec((K, K), lambda i: (0, 0)),
            pl.BlockSpec((K, K), lambda i: (0, 0)),
            pl.BlockSpec((K, STEP), lambda i: (0, i)),
        ],
        out_specs=pl.BlockSpec((STEP, K), lambda i: (i, 0)),
        scratch_shapes=[pltpu.VMEM((K, K), bf16)] * 2,
        cost_estimate=pl.CostEstimate(
            flops=9 * 2 * K**3, bytes_accessed=6 << 20, transcendentals=0
        ),
    )(at, w, p, d)


def gather(block, axis, n):
    out = lax.all_to_all(jnp.broadcast_to(block[None], (n,) + block.shape), axis, 0, 0)
    return out.reshape((-1,) + block.shape[1:])


def on_device(pivots, demand, prices):
    z, core, y, x = (lax.axis_index(name) for name in ("z", "core", "y", "x"))
    at = jnp.stack([z, core, y, x, pivots[0], pivots[1]]).astype(jnp.int32)
    flat = demand.T
    prices_all = lax.all_gather(prices, ROW, axis=0, tiled=True)
    demand_all = lax.all_gather(gather(flat, "x", NX), "y", axis=0, tiled=True)
    price_cut, demand_cut = small(cut_kernel, ((128, 128), (64, 128)), at, prices, flat)
    price_rows = lax.all_to_all(price_cut.reshape(32, 4, 128), COL, 0, 0)
    demand_rows = lax.all_to_all(demand_cut.reshape(16, 4, 128), ROW, 0, 0)
    (packed,) = small(
        pick_kernel, ((64, 128),), at, price_rows.reshape(128, 128), demand_rows.reshape(64, 128)
    )
    packed = lax.all_to_all(packed.reshape(NZ, 8, 128), "z", 0, 0).reshape(NZ * 8, 128)
    packed = gather(gather(packed, "y", NY), "x", NX)
    w = invert(at, packed, lax.ppermute(packed, "core", flip(NCORE, 1)))
    return tile(at, w, prices_all, demand_all)


def solution(mesh):
    inner = Mesh(mesh.devices.reshape(NZ, NCORE, NY, NX), ROW + COL)
    placed = (P(), P(ROW, COL), P(ROW, COL))
    return jax.shard_map(
        on_device, mesh=inner, in_specs=placed, out_specs=P(ROW, COL), check_vma=False
    )
```

```python
import jax
import jax.numpy as jnp
from jax import lax
from jax.experimental import pallas as pl
from jax.experimental.pallas import tpu as pltpu
from jax.sharding import Mesh
from jax.sharding import PartitionSpec as P

PW = 256
K = 512
FAST, GAIN = 4, 1.85
VMEM = 20 << 20
NZ, NCORE, NY, NX = 8, 2, 8, 4
ROW = ("z", "core")
COL = ("y", "x")


def flip(n, bit):
    return [(i, i ^ bit) for i in range(n)]


def split(a):
    high = a.astype(jnp.bfloat16)
    return high, (a - high.astype(jnp.float32)).astype(jnp.bfloat16)


def dot1(a, b):
    return jnp.dot(a, b, preferred_element_type=jnp.float32)


def dot1_t(a, b):
    return lax.dot_general(
        a, b, (((1,), (1,)), ((), ())), preferred_element_type=jnp.float32
    )


def dot3(a, b, dot=dot1):
    return dot(a[0], b[0]) + (dot(a[0], b[1]) + dot(a[1], b[0]))


def eye(rows, cols):
    r = lax.broadcasted_iota(jnp.int32, (rows, cols), 0)
    c = lax.broadcasted_iota(jnp.int32, (rows, cols), 1)
    return (r == c).astype(jnp.float32)


def cut_kernel(at, p_ref, d_ref, pp_ref, dp_ref):
    for q in range(4):
        pivot = at[4 + q // 2]
        start = pl.multiple_of((pivot & 1) * PW + (q % 2) * 128, 128)
        pp_ref[pl.ds(q, 32, stride=4), :] = p_ref[:, pl.ds(start, 128)]
        start = pl.multiple_of((pivot & 3) * PW + (q % 2) * 128, 128)
        dp_ref[pl.ds(q, 16, stride=4), :] = d_ref[:, pl.ds(start, 128)]


def pick_kernel(at, p_ref, d_ref, o_ref):
    row = lax.broadcasted_iota(jnp.int32, (8, 128), 0)
    packed = jnp.zeros((8, 128), jnp.float32)
    for q in range(4):
        pivot = at[4 + q // 2]
        packed = jnp.where(row == q, p_ref[pl.ds(4 * (pivot // 2) + q, 1), :], packed)
        packed = jnp.where(row == 4 + q, d_ref[pl.ds(4 * (pivot // 4) + q, 1), :], packed)
    for k in range(NZ):
        o_ref[pl.ds(8 * k, 8), :] = packed


def small(kernel, shapes, at, *parts):
    return pl.pallas_call(
        kernel,
        out_shape=[jax.ShapeDtypeStruct(shape, jnp.float32) for shape in shapes],
        in_specs=[pl.BlockSpec(memory_space=pltpu.SMEM)]
        + [pl.BlockSpec(memory_space=pltpu.VMEM)] * len(parts),
        out_specs=[pl.BlockSpec(memory_space=pltpu.VMEM)] * len(shapes),
        compiler_params=pltpu.CompilerParams(vmem_limit_bytes=VMEM),
    )(at, *parts)


def slab_row(n, of_prices):
    row = 2 * (n & 7) + (n >> 8)
    col = 4 * ((n >> 3) & 7) + ((n >> 6) & 3)
    return 32 * row + col if of_prices else 16 * col + row


def invert_kernel(
    at, own, other, slab, vh_ref, vl_ref, x_ref, b_ref, bh_ref, bl_ref, pj_ref, dj_ref
):
    core, y, x, first, second = (at[i] for i in range(1, 6))
    for ref, side in ((own, core), (other, 1 - core)):
        to = pl.ds(pl.multiple_of(side * 256, 256), 256)
        for q in range(4):
            pj_ref[to, 128 * q : 128 * q + 128] = ref[pl.ds(q, 256, stride=8), :]
            dj_ref[to, 128 * q : 128 * q + 128] = ref[pl.ds(q + 4, 256, stride=8), :]
    n0 = lax.broadcasted_iota(jnp.int32, (K, 128), 0)
    n1 = lax.broadcasted_iota(jnp.int32, (8, K), 1)

    def match(down, across):
        down, across = jnp.concatenate([down] * 4, 1), jnp.concatenate([across] * 64, 0)
        return (down == across).astype(jnp.float32)

    b = match(slab_row(n0, True), slab_row(n1, False)) - dot3(split(pj_ref[...]), split(dj_ref[...]), dot1_t)
    b_ref[...] = b
    size = jnp.max(jnp.sum(jnp.abs(b), axis=0)) * jnp.max(jnp.sum(jnp.abs(b), axis=1))
    bh, bl = split(b)
    bh_ref[...] = bh
    bl_ref[...] = bl
    x_ref[...] = b.T / size

    def coarse_step(gain, measured):
        xv = x_ref[...]
        xh = xv.astype(jnp.bfloat16)
        r = eye(K, K) - dot1(bh_ref[...], xh)
        xv = xv + dot1(xh, r.astype(jnp.bfloat16))
        x_ref[...] = xv * gain if gain != 1.0 else xv
        return jnp.sum(r * r) if measured else None

    for _ in range(FAST):
        coarse_step(GAIN, False)

    def coarse(carry):
        coarse_step(1.0, False)
        return carry[0] + 1, coarse_step(1.0, True)

    lax.while_loop(
        lambda c: (c[0] < 20) & (c[1] > 0.3) & (c[1] < 4.0 * K),
        coarse,
        (jnp.int32(0), jnp.float32(K)),
    )

    def fine(carry):
        count, last, _ = carry
        xv = x_ref[...]
        xs = split(xv)
        r = eye(K, K) - dot3((bh_ref[...], bl_ref[...]), xs)
        now = jnp.sum(r * r)
        lost = (count == 0) & jnp.logical_not(now < K)
        x_ref[...] = xv + dot1(xs[0], r.astype(jnp.bfloat16))

        @pl.when(lost)
        def _():
            x_ref[...] = b_ref[...].T / size

        stuck = (now > 0.25 * last) & (now < 0.1)
        return count + 1, now, lost | ((now > 1e-5) & jnp.logical_not(stuck))

    lax.while_loop(
        lambda c: (c[0] < 60) & c[2],
        fine,
        (jnp.int32(0), jnp.float32(8.0 * K), jnp.bool_(True)),
    )

    spread = jnp.sum(b_ref[...] * b_ref[...]) * jnp.sum(x_ref[...] * x_ref[...])

    @pl.when(spread > 2e6)
    def _():
        xv = x_ref[...]
        r = eye(K, K) - jnp.dot(
            b_ref[...], xv, precision=lax.Precision.HIGHEST, preferred_element_type=jnp.float32
        )
        x_ref[...] = xv + dot3(split(xv), split(r))

    order = match(slab_row(n0, True), n1).astype(jnp.bfloat16)
    sh, sl = split(slab[...])
    rows = dot1(order, sh).astype(jnp.bfloat16), dot1(order, sl).astype(jnp.bfloat16)
    v = dot3(split(x_ref[...]), rows)
    col = lax.broadcasted_iota(jnp.int32, (1, K), 1) + (y * NX + x) * K
    gone = (col // PW == first) | (col // PW == second)
    vh, vl = split(jnp.where(gone, 0.0, v))
    order = match(n0, slab_row(n1, False)).astype(jnp.bfloat16)
    vh_ref[...] = dot1(order, vh).astype(jnp.bfloat16)
    vl_ref[...] = dot1(order, vl).astype(jnp.bfloat16)


def invert(at, own, other, slab):
    f32, bf16 = jnp.float32, jnp.bfloat16
    return pl.pallas_call(
        invert_kernel,
        out_shape=[jax.ShapeDtypeStruct((K, K), bf16)] * 2,
        in_specs=[pl.BlockSpec(memory_space=pltpu.SMEM)]
        + [pl.BlockSpec(memory_space=pltpu.VMEM)] * 3,
        out_specs=[pl.BlockSpec(memory_space=pltpu.VMEM)] * 2,
        scratch_shapes=[pltpu.VMEM((K, K), f32)] * 2
        + [pltpu.VMEM((K, K), bf16)] * 2
        + [pltpu.VMEM((K, K), f32)] * 2,
        compiler_params=pltpu.CompilerParams(vmem_limit_bytes=VMEM),
        cost_estimate=pl.CostEstimate(
            flops=60 * 2 * K**3, bytes_accessed=5 << 20, transcendentals=0
        ),
    )(at, own, other, slab)


STEP = 256


def tile_kernel(at, vh_ref, vl_ref, d_ref, o_ref):
    z, core, y, x, first, second = (at[i] for i in range(6))
    base = (z * NCORE + core) * 1024 + pl.program_id(0) * STEP
    d = split(d_ref[...].T)
    row = lax.broadcasted_iota(jnp.int32, (STEP, 1), 0) + base
    col = lax.broadcasted_iota(jnp.int32, (1, K), 1) + (y * NX + x) * K
    kept = (base // PW != first) & (base // PW != second)
    gone = (col // PW == first) | (col // PW == second)
    tile = ((row == col) & jnp.logical_not(gone)).astype(jnp.float32)
    tile = tile - dot3(d, (vh_ref[...], vl_ref[...]))
    o_ref[...] = jnp.where(kept, tile, 0.0)


def tile(at, vh, vl, d):
    rows = d.shape[1]
    return pl.pallas_call(
        tile_kernel,
        grid=(rows // STEP,),
        out_shape=jax.ShapeDtypeStruct((rows, K), jnp.float32),
        in_specs=[
            pl.BlockSpec(memory_space=pltpu.SMEM),
            pl.BlockSpec((K, K), lambda i: (0, 0)),
            pl.BlockSpec((K, K), lambda i: (0, 0)),
            pl.BlockSpec((K, STEP), lambda i: (0, i)),
        ],
        out_specs=pl.BlockSpec((STEP, K), lambda i: (i, 0)),
        compiler_params=pltpu.CompilerParams(vmem_limit_bytes=VMEM),
        cost_estimate=pl.CostEstimate(
            flops=6 * 2 * K**3, bytes_accessed=6 << 20, transcendentals=0
        ),
    )(at, vh, vl, d)


def gather(block, axis, n):
    out = lax.all_to_all(jnp.broadcast_to(block[None], (n,) + block.shape), axis, 0, 0)
    return out.reshape((-1,) + block.shape[1:])


def on_device(pivots, demand, prices):
    z, core, y, x = (lax.axis_index(name) for name in ("z", "core", "y", "x"))
    at = jnp.stack([z, core, y, x, pivots[0], pivots[1]]).astype(jnp.int32)
    flat = demand.T
    prices_all = lax.all_gather(prices, ROW, axis=0, tiled=True)
    demand_all = lax.all_gather(gather(flat, "x", NX), "y", axis=0, tiled=True)
    price_cut, demand_cut = small(cut_kernel, ((128, 128), (64, 128)), at, prices, flat)
    price_rows = lax.all_to_all(price_cut.reshape(32, 4, 128), COL, 0, 0)
    demand_rows = lax.all_to_all(demand_cut.reshape(16, 4, 128), ROW, 0, 0)
    (packed,) = small(
        pick_kernel, ((64, 128),), at, price_rows.reshape(128, 128), demand_rows.reshape(64, 128)
    )
    packed = lax.all_to_all(packed.reshape(NZ, 8, 128), "z", 0, 0).reshape(NZ * 8, 128)
    packed = gather(gather(packed, "y", NY), "x", NX)
    vh, vl = invert(at, packed, lax.ppermute(packed, "core", flip(NCORE, 1)), prices_all)
    return tile(at, vh, vl, demand_all)


def solution(mesh):
    inner = Mesh(mesh.devices.reshape(NZ, NCORE, NY, NX), ROW + COL)
    placed = (P(), P(ROW, COL), P(ROW, COL))
    return jax.shard_map(
        on_device, mesh=inner, in_specs=placed, out_specs=P(ROW, COL), check_vma=False
    )
```

```python
import jax
import jax.numpy as jnp
from jax import lax
from jax.experimental import pallas as pl
from jax.experimental.pallas import tpu as pltpu
from jax.sharding import Mesh
from jax.sharding import PartitionSpec as P

PW = 256
K = 512
FAST, GAIN = 4, 1.85
VMEM = 20 << 20
NZ, NCORE, NY, NX = 8, 2, 8, 4
ROW = ("z", "core")
COL = ("y", "x")


def flip(n, bit):
    return [(i, i ^ bit) for i in range(n)]


def split(a):
    high = a.astype(jnp.bfloat16)
    return high, (a - high.astype(jnp.float32)).astype(jnp.bfloat16)


def dot1(a, b):
    return jnp.dot(a, b, preferred_element_type=jnp.float32)


def dot1_t(a, b):
    return lax.dot_general(
        a, b, (((1,), (1,)), ((), ())), preferred_element_type=jnp.float32
    )


def dot3(a, b, dot=dot1):
    return dot(a[0], b[0]) + (dot(a[0], b[1]) + dot(a[1], b[0]))


def eye(rows, cols):
    r = lax.broadcasted_iota(jnp.int32, (rows, cols), 0)
    c = lax.broadcasted_iota(jnp.int32, (rows, cols), 1)
    return (r == c).astype(jnp.float32)


PART = 160


def cut_kernel(at, p_ref, d_ref, px_ref, dp_ref, pp_ref):
    pivots = at[4], at[5]
    for q in range(4):
        pivot = pivots[q // 2]
        start = pl.multiple_of((pivot & 1) * PW + (q % 2) * 128, 128)
        piece = p_ref[:, pl.ds(start, 128)]
        pp_ref[pl.ds(q, 32, stride=4), :] = piece
        start = pl.multiple_of((pivot & 3) * PW + (q % 2) * 128, 128)
        dp_ref[pl.ds(q, 16, stride=4), :] = d_ref[:, pl.ds(start, 128)]
    for k in range(NX):
        for y in range(NY):
            px_ref[pl.ds(k * PART + 4 * y, 4), :] = pp_ref[pl.ds(4 * (4 * y + k), 4), :]
        for t in range(8):
            px_ref[pl.ds(k * PART + 32 + 16 * t, 16), :] = d_ref[:, 128 * t : 128 * t + 128]


def sift_kernel(at, px_ref, py_ref, d_ref):
    pivots = at[4], at[5]
    row = lax.broadcasted_iota(jnp.int32, (32, 128), 0) & 3
    first = px_ref[pl.ds(pl.multiple_of(((pivots[0] // 2) & 3) * PART, 8), 32), :]
    second = px_ref[pl.ds(pl.multiple_of(((pivots[1] // 2) & 3) * PART, 8), 32), :]
    py_ref[...] = jnp.where(row < 2, first, second)
    for k in range(NX):
        d_ref[pl.ds(128 * k, 128), :] = px_ref[pl.ds(k * PART + 32, 128), :]


def pick_kernel(at, p_ref, d_ref, o_ref):
    pivots = at[4], at[5]
    row = lax.broadcasted_iota(jnp.int32, (8, 128), 0)
    packed = jnp.zeros((8, 128), jnp.float32)
    for q in range(4):
        pivot = pivots[q // 2]
        packed = jnp.where(row == q, p_ref[pl.ds(4 * (pivot // 8) + q, 1), :], packed)
        packed = jnp.where(row == 4 + q, d_ref[pl.ds(4 * (pivot // 4) + q, 1), :], packed)
    for k in range(NZ):
        o_ref[pl.ds(8 * k, 8), :] = packed


def small(kernel, shapes, at, *parts):
    return pl.pallas_call(
        kernel,
        out_shape=[jax.ShapeDtypeStruct(shape, jnp.float32) for shape in shapes],
        in_specs=[pl.BlockSpec(memory_space=pltpu.SMEM)]
        + [pl.BlockSpec(memory_space=pltpu.VMEM)] * len(parts),
        out_specs=[pl.BlockSpec(memory_space=pltpu.VMEM)] * len(shapes),
        compiler_params=pltpu.CompilerParams(vmem_limit_bytes=VMEM),
    )(at, *parts)


def slab_row(n, of_prices):
    row = 2 * (n & 7) + (n >> 8)
    col = 4 * ((n >> 3) & 7) + ((n >> 6) & 3)
    return 32 * row + col if of_prices else 16 * col + row


def invert_kernel(
    at, own, other, slab, vh_ref, vl_ref, x_ref, b_ref, bh_ref, bl_ref, pj_ref, dj_ref
):
    core, y, x, first, second = (at[i] for i in range(1, 6))
    for ref, side in ((own, core), (other, 1 - core)):
        to = pl.ds(pl.multiple_of(side * 256, 256), 256)
        for q in range(4):
            pj_ref[to, 128 * q : 128 * q + 128] = ref[pl.ds(q, 256, stride=8), :]
            dj_ref[to, 128 * q : 128 * q + 128] = ref[pl.ds(q + 4, 256, stride=8), :]
    n0 = lax.broadcasted_iota(jnp.int32, (K, 128), 0)
    n1 = lax.broadcasted_iota(jnp.int32, (8, K), 1)

    def match(down, across):
        down, across = jnp.concatenate([down] * 4, 1), jnp.concatenate([across] * 64, 0)
        return (down == across).astype(jnp.float32)

    b = match(slab_row(n0, True), slab_row(n1, False)) - dot3(split(pj_ref[...]), split(dj_ref[...]), dot1_t)
    b_ref[...] = b
    size = jnp.max(jnp.sum(jnp.abs(b), axis=0)) * jnp.max(jnp.sum(jnp.abs(b), axis=1))
    bh, bl = split(b)
    bh_ref[...] = bh
    bl_ref[...] = bl
    x_ref[...] = b.T / size

    def coarse_step(gain, measured):
        xv = x_ref[...]
        xh = xv.astype(jnp.bfloat16)
        r = eye(K, K) - dot1(bh_ref[...], xh)
        xv = xv + dot1(xh, r.astype(jnp.bfloat16))
        x_ref[...] = xv * gain if gain != 1.0 else xv
        return jnp.sum(r * r) if measured else None

    for _ in range(FAST):
        coarse_step(GAIN, False)

    def coarse(carry):
        coarse_step(1.0, False)
        return carry[0] + 1, coarse_step(1.0, True)

    lax.while_loop(
        lambda c: (c[0] < 20) & (c[1] > 0.3) & (c[1] < 4.0 * K),
        coarse,
        (jnp.int32(0), jnp.float32(K)),
    )

    def fine(carry):
        count, last, _ = carry
        xv = x_ref[...]
        xs = split(xv)
        r = eye(K, K) - dot3((bh_ref[...], bl_ref[...]), xs)
        now = jnp.sum(r * r)
        lost = (count == 0) & jnp.logical_not(now < K)
        x_ref[...] = xv + dot1(xs[0], r.astype(jnp.bfloat16))

        @pl.when(lost)
        def _():
            x_ref[...] = b_ref[...].T / size

        stuck = (now > 0.25 * last) & (now < 0.1)
        return count + 1, now, lost | ((now > 1e-5) & jnp.logical_not(stuck))

    lax.while_loop(
        lambda c: (c[0] < 60) & c[2],
        fine,
        (jnp.int32(0), jnp.float32(8.0 * K), jnp.bool_(True)),
    )

    spread = jnp.sum(b_ref[...] * b_ref[...]) * jnp.sum(x_ref[...] * x_ref[...])

    @pl.when(spread > 2e6)
    def _():
        xv = x_ref[...]
        r = eye(K, K) - jnp.dot(
            b_ref[...], xv, precision=lax.Precision.HIGHEST, preferred_element_type=jnp.float32
        )
        x_ref[...] = xv + dot3(split(xv), split(r))

    order = match(slab_row(n0, True), n1).astype(jnp.bfloat16)
    sh, sl = split(slab[...])
    rows = dot1(order, sh).astype(jnp.bfloat16), dot1(order, sl).astype(jnp.bfloat16)
    v = dot3(split(x_ref[...]), rows)
    col = lax.broadcasted_iota(jnp.int32, (1, K), 1) + (y * NX + x) * K
    gone = (col // PW == first) | (col // PW == second)
    vh, vl = split(jnp.where(gone, 0.0, v))
    order = match(n0, slab_row(n1, False)).astype(jnp.bfloat16)
    vh_ref[...] = dot1(order, vh).astype(jnp.bfloat16)
    vl_ref[...] = dot1(order, vl).astype(jnp.bfloat16)


def invert(at, own, other, slab):
    f32, bf16 = jnp.float32, jnp.bfloat16
    return pl.pallas_call(
        invert_kernel,
        out_shape=[jax.ShapeDtypeStruct((K, K), bf16)] * 2,
        in_specs=[pl.BlockSpec(memory_space=pltpu.SMEM)]
        + [pl.BlockSpec(memory_space=pltpu.VMEM)] * 3,
        out_specs=[pl.BlockSpec(memory_space=pltpu.VMEM)] * 2,
        scratch_shapes=[pltpu.VMEM((K, K), f32)] * 2
        + [pltpu.VMEM((K, K), bf16)] * 2
        + [pltpu.VMEM((K, K), f32)] * 2,
        compiler_params=pltpu.CompilerParams(vmem_limit_bytes=VMEM),
        cost_estimate=pl.CostEstimate(
            flops=60 * 2 * K**3, bytes_accessed=5 << 20, transcendentals=0
        ),
    )(at, own, other, slab)


STEP = 256


def tile_kernel(at, vh_ref, vl_ref, d_ref, o_ref):
    z, core, y, x, first, second = (at[i] for i in range(6))
    base = (z * NCORE + core) * 1024 + pl.program_id(0) * STEP
    d = split(
        jnp.concatenate([d_ref[:, t].reshape(K, 128).T for t in range(STEP // 128)], 0)
    )
    row = lax.broadcasted_iota(jnp.int32, (STEP, 1), 0) + base
    col = lax.broadcasted_iota(jnp.int32, (1, K), 1) + (y * NX + x) * K
    kept = (base // PW != first) & (base // PW != second)
    gone = (col // PW == first) | (col // PW == second)
    tile = ((row == col) & jnp.logical_not(gone)).astype(jnp.float32)
    tile = tile - dot3(d, (vh_ref[...], vl_ref[...]))
    o_ref[...] = jnp.where(kept, tile, 0.0)


def tile(at, vh, vl, d):
    rows = 128 * d.shape[1]
    return pl.pallas_call(
        tile_kernel,
        grid=(rows // STEP,),
        out_shape=jax.ShapeDtypeStruct((rows, K), jnp.float32),
        in_specs=[
            pl.BlockSpec(memory_space=pltpu.SMEM),
            pl.BlockSpec((K, K), lambda i: (0, 0)),
            pl.BlockSpec((K, K), lambda i: (0, 0)),
            pl.BlockSpec((32, STEP // 128, 16, 128), lambda i: (0, i, 0, 0)),
        ],
        out_specs=pl.BlockSpec((STEP, K), lambda i: (i, 0)),
        compiler_params=pltpu.CompilerParams(vmem_limit_bytes=VMEM),
        cost_estimate=pl.CostEstimate(
            flops=6 * 2 * K**3, bytes_accessed=6 << 20, transcendentals=0
        ),
    )(at, vh, vl, d)


def gather(block, axis, n):
    out = lax.all_to_all(jnp.broadcast_to(block[None], (n,) + block.shape), axis, 0, 0)
    return out.reshape((-1,) + block.shape[1:])


def on_device(pivots, demand, prices):
    z, core, y, x = (lax.axis_index(name) for name in ("z", "core", "y", "x"))
    at = jnp.stack([z, core, y, x, pivots[0], pivots[1]]).astype(jnp.int32)
    prices_all = lax.all_gather(prices, ROW, axis=0, tiled=True)
    price_cut, demand_cut, _ = small(
        cut_kernel, ((NX * PART, 128), (64, 128), (128, 128)), at, prices, demand.T
    )
    price_cut = lax.all_to_all(price_cut.reshape(NX, PART, 128), "x", 0, 0)
    price_cut, demand_part = small(
        sift_kernel, ((32, 128), (512, 128)), at, price_cut.reshape(NX * PART, 128)
    )
    demand_all = lax.all_gather(demand_part, "y", axis=0, tiled=True)
    price_rows = lax.all_to_all(price_cut.reshape(NY, 4, 128), "y", 0, 0)
    demand_rows = lax.all_to_all(demand_cut.reshape(16, 4, 128), ROW, 0, 0)
    (packed,) = small(
        pick_kernel, ((64, 128),), at,
        price_rows.reshape(32, 128), demand_rows.reshape(64, 128),
    )
    packed = lax.all_to_all(packed.reshape(NZ, 8, 128), "z", 0, 0).reshape(NZ * 8, 128)
    packed = gather(gather(packed, "y", NY), "x", NX)
    vh, vl = invert(at, packed, lax.ppermute(packed, "core", flip(NCORE, 1)), prices_all)
    return tile(at, vh, vl, demand_all.reshape(NY * NX, 8, 16, 128))


def solution(mesh):
    inner = Mesh(mesh.devices.reshape(NZ, NCORE, NY, NX), ROW + COL)
    placed = (P(), P(ROW, COL), P(ROW, COL))
    return jax.shard_map(
        on_device, mesh=inner, in_specs=placed, out_specs=P(ROW, COL), check_vma=False
    )
```

```python
import jax
import jax.numpy as jnp
from jax import lax
from jax.experimental import pallas as pl
from jax.experimental.pallas import tpu as pltpu
from jax.sharding import Mesh
from jax.sharding import PartitionSpec as P

PW = 256
K = 512
FAST, GAIN = 4, 1.85
VMEM = 20 << 20
NZ, NCORE, NY, NX = 8, 2, 8, 4
ROW = ("z", "core")
COL = ("y", "x")


def flip(n, bit):
    return [(i, i ^ bit) for i in range(n)]


def split(a):
    high = a.astype(jnp.bfloat16)
    return high, (a - high.astype(jnp.float32)).astype(jnp.bfloat16)


def dot1(a, b):
    return jnp.dot(a, b, preferred_element_type=jnp.float32)


def dot1_t(a, b):
    return lax.dot_general(
        a, b, (((1,), (1,)), ((), ())), preferred_element_type=jnp.float32
    )


def dot3(a, b, dot=dot1):
    return dot(a[0], b[0]) + (dot(a[0], b[1]) + dot(a[1], b[0]))


def eye(rows, cols):
    r = lax.broadcasted_iota(jnp.int32, (rows, cols), 0)
    c = lax.broadcasted_iota(jnp.int32, (rows, cols), 1)
    return (r == c).astype(jnp.float32)


PART = 160


def cut_kernel(at, p_ref, d_ref, px_ref, dp_ref, pp_ref, dd_ref):
    for q in range(4):
        pivot = at[4 + q // 2]
        start = pl.multiple_of((pivot & 1) * PW + (q % 2) * 128, 128)
        pp_ref[pl.ds(q, 32, stride=4), :] = p_ref[:, pl.ds(start, 128)]
        start = pl.multiple_of((pivot & 3) * PW + (q % 2) * 128, 128)
        dd_ref[pl.ds(q, 16, stride=4), :] = d_ref[:, pl.ds(start, 128)]
    for i in range(16):
        dp_ref[pl.ds(4 * (8 * (i % 2) + i // 2), 4), :] = dd_ref[pl.ds(4 * i, 4), :]
    for k in range(NX):
        for y in range(NY):
            px_ref[pl.ds(k * PART + 4 * y, 4), :] = pp_ref[pl.ds(4 * (4 * y + k), 4), :]
        for t in range(8):
            px_ref[pl.ds(k * PART + 32 + 16 * t, 16), :] = d_ref[:, 128 * t : 128 * t + 128]


def sift_kernel(at, px_ref, dp_ref, twin_ref, py_ref, dz_ref, d_ref):
    row = lax.broadcasted_iota(jnp.int32, (32, 128), 0) & 3
    core = at[1]
    price, mine = [], []
    for which in range(2):
        pivot = at[4 + which]
        start = pl.multiple_of(((pivot // 2) & 3) * PART, 8)
        price.append(px_ref[pl.ds(start, 32), :])
        mine.append(((pivot // 4) & 1) == core)
    py_ref[...] = jnp.where(row < 2, price[0], price[1])
    half = pl.ds(pl.multiple_of(core * 32, 32), 32)
    own, twin = dp_ref[half, :], twin_ref[half, :]
    kept = jnp.where(
        row < 2, jnp.where(mine[0], own, twin), jnp.where(mine[1], own, twin)
    )
    for k in range(NZ):
        dz_ref[pl.ds(32 * k, 32), :] = kept
    for k in range(NX):
        d_ref[pl.ds(128 * k, 128), :] = px_ref[pl.ds(k * PART + 32, 128), :]


def pick_z_kernel(at, py_ref, dz_ref, o_ref):
    row = lax.broadcasted_iota(jnp.int32, (32, 128), 0) & 3
    parts = [dz_ref[pl.ds(pl.multiple_of((at[4 + w] // 8) * 32, 32), 32), :] for w in range(2)]
    kept = jnp.where(row < 2, parts[0], parts[1])
    for k in range(NY):
        o_ref[pl.ds(64 * k, 32), :] = py_ref[...]
        o_ref[pl.ds(64 * k + 32, 32), :] = kept


def pick_y_kernel(at, y_ref, pz_ref, dx_ref):
    row = lax.broadcasted_iota(jnp.int32, (32, 128), 0) & 3
    parts = [y_ref[pl.ds(pl.multiple_of((at[4 + w] // 8) * 64, 64), 32), :] for w in range(2)]
    kept = jnp.where(row < 2, parts[0], parts[1])
    for k in range(NZ):
        pz_ref[pl.ds(32 * k, 32), :] = kept
    for k in range(NY):
        dx_ref[pl.ds(32 * k, 32), :] = y_ref[pl.ds(64 * k + 32, 32), :]


def join_kernel(at, pz_ref, dx_ref, o_ref):
    for k in range(NX):
        o_ref[pl.ds(512 * k, 256), :] = pz_ref[...]
        o_ref[pl.ds(512 * k + 256, 256), :] = dx_ref[...]


def small(kernel, shapes, at, *parts):
    return pl.pallas_call(
        kernel,
        out_shape=[jax.ShapeDtypeStruct(shape, jnp.float32) for shape in shapes],
        in_specs=[pl.BlockSpec(memory_space=pltpu.SMEM)]
        + [pl.BlockSpec(memory_space=pltpu.VMEM)] * len(parts),
        out_specs=[pl.BlockSpec(memory_space=pltpu.VMEM)] * len(shapes),
        compiler_params=pltpu.CompilerParams(vmem_limit_bytes=VMEM),
    )(at, *parts)


def slab_row(n, of_prices):
    core, x, high, low = n >> 8, (n >> 6) & 3, (n >> 3) & 7, n & 7
    if of_prices:
        return 64 * high + 32 * core + 4 * low + x
    return 64 * high + 16 * x + 2 * low + core


def invert_kernel(
    at, own, other, slab, vh_ref, vl_ref, x_ref, b_ref, bh_ref, bl_ref, pj_ref, dj_ref,
    slab_ref, sem,
):
    core, y, x, first, second = (at[i] for i in range(1, 6))
    fetch = pltpu.make_async_copy(slab, slab_ref, sem)
    fetch.start()
    for ref, side in ((own, core), (other, 1 - core)):
        for k in range(NX):
            to = pl.ds(pl.multiple_of(side * 256 + 64 * k, 64), 64)
            for q in range(4):
                lanes = slice(128 * q, 128 * q + 128)
                pj_ref[to, lanes] = ref[pl.ds(512 * k + q, 64, stride=4), :]
                dj_ref[to, lanes] = ref[pl.ds(512 * k + 256 + q, 64, stride=4), :]
    n0 = lax.broadcasted_iota(jnp.int32, (K, 128), 0)
    n1 = lax.broadcasted_iota(jnp.int32, (8, K), 1)

    def match(down, across):
        down, across = jnp.concatenate([down] * 4, 1), jnp.concatenate([across] * 64, 0)
        return (down == across).astype(jnp.float32)

    b = match(slab_row(n0, True), slab_row(n1, False)) - dot3(split(pj_ref[...]), split(dj_ref[...]), dot1_t)
    b_ref[...] = b
    size = jnp.max(jnp.sum(jnp.abs(b), axis=0)) * jnp.max(jnp.sum(jnp.abs(b), axis=1))
    bh, bl = split(b)
    bh_ref[...] = bh
    bl_ref[...] = bl
    x_ref[...] = b.T / size

    def coarse_step(gain, measured):
        xv = x_ref[...]
        xh = xv.astype(jnp.bfloat16)
        r = eye(K, K) - dot1(bh_ref[...], xh)
        xv = xv + dot1(xh, r.astype(jnp.bfloat16))
        x_ref[...] = xv * gain if gain != 1.0 else xv
        return jnp.sum(r * r) if measured else None

    for _ in range(FAST):
        coarse_step(GAIN, False)

    def coarse(carry):
        coarse_step(1.0, False)
        return carry[0] + 1, coarse_step(1.0, True)

    lax.while_loop(
        lambda c: (c[0] < 20) & (c[1] > 0.3) & (c[1] < 4.0 * K),
        coarse,
        (jnp.int32(0), jnp.float32(K)),
    )

    def fine(carry):
        count, last, _ = carry
        xv = x_ref[...]
        xs = split(xv)
        r = eye(K, K) - dot3((bh_ref[...], bl_ref[...]), xs)
        now = jnp.sum(r * r)
        lost = (count == 0) & jnp.logical_not(now < K)
        x_ref[...] = xv + dot1(xs[0], r.astype(jnp.bfloat16))

        @pl.when(lost)
        def _():
            x_ref[...] = b_ref[...].T / size

        stuck = (now > 0.25 * last) & (now < 0.1)
        return count + 1, now, lost | ((now > 1e-5) & jnp.logical_not(stuck))

    lax.while_loop(
        lambda c: (c[0] < 60) & c[2],
        fine,
        (jnp.int32(0), jnp.float32(8.0 * K), jnp.bool_(True)),
    )

    spread = jnp.sum(b_ref[...] * b_ref[...]) * jnp.sum(x_ref[...] * x_ref[...])

    @pl.when(spread > 2e6)
    def _():
        xv = x_ref[...]
        r = eye(K, K) - jnp.dot(
            b_ref[...], xv, precision=lax.Precision.HIGHEST, preferred_element_type=jnp.float32
        )
        x_ref[...] = xv + dot3(split(xv), split(r))

    order = match(slab_row(n0, True), n1).astype(jnp.bfloat16)
    fetch.wait()
    sh, sl = split(slab_ref[...])
    rows = dot1(order, sh).astype(jnp.bfloat16), dot1(order, sl).astype(jnp.bfloat16)
    v = dot3(split(x_ref[...]), rows)
    col = lax.broadcasted_iota(jnp.int32, (1, K), 1) + (y * NX + x) * K
    gone = (col // PW == first) | (col // PW == second)
    vh, vl = split(jnp.where(gone, 0.0, v))
    order = match(n0, slab_row(n1, False)).astype(jnp.bfloat16)
    vh_ref[...] = dot1(order, vh).astype(jnp.bfloat16)
    vl_ref[...] = dot1(order, vl).astype(jnp.bfloat16)


def invert(at, own, other, slab):
    f32, bf16 = jnp.float32, jnp.bfloat16
    return pl.pallas_call(
        invert_kernel,
        out_shape=[jax.ShapeDtypeStruct((K, K), bf16)] * 2,
        in_specs=[pl.BlockSpec(memory_space=pltpu.SMEM)]
        + [pl.BlockSpec(memory_space=pltpu.VMEM)] * 2
        + [pl.BlockSpec(memory_space=pltpu.HBM)],
        out_specs=[pl.BlockSpec(memory_space=pltpu.VMEM)] * 2,
        scratch_shapes=[pltpu.VMEM((K, K), f32)] * 2
        + [pltpu.VMEM((K, K), bf16)] * 2
        + [pltpu.VMEM((K, K), f32)] * 3
        + [pltpu.SemaphoreType.DMA],
        compiler_params=pltpu.CompilerParams(vmem_limit_bytes=VMEM),
        cost_estimate=pl.CostEstimate(
            flops=60 * 2 * K**3, bytes_accessed=5 << 20, transcendentals=0
        ),
    )(at, own, other, slab)


STEP = 256


def tile_kernel(at, vh_ref, vl_ref, d_ref, o_ref):
    z, core, y, x, first, second = (at[i] for i in range(6))
    base = (z * NCORE + core) * 1024 + pl.program_id(0) * STEP
    d = split(
        jnp.concatenate([d_ref[:, t].reshape(K, 128).T for t in range(STEP // 128)], 0)
    )
    row = lax.broadcasted_iota(jnp.int32, (STEP, 1), 0) + base
    col = lax.broadcasted_iota(jnp.int32, (1, K), 1) + (y * NX + x) * K
    kept = (base // PW != first) & (base // PW != second)
    gone = (col // PW == first) | (col // PW == second)
    tile = ((row == col) & jnp.logical_not(gone)).astype(jnp.float32)
    tile = tile - dot3(d, (vh_ref[...], vl_ref[...]))
    o_ref[...] = jnp.where(kept, tile, 0.0)


def tile(at, vh, vl, d):
    rows = 128 * d.shape[1]
    return pl.pallas_call(
        tile_kernel,
        grid=(rows // STEP,),
        out_shape=jax.ShapeDtypeStruct((rows, K), jnp.float32),
        in_specs=[
            pl.BlockSpec(memory_space=pltpu.SMEM),
            pl.BlockSpec((K, K), lambda i: (0, 0)),
            pl.BlockSpec((K, K), lambda i: (0, 0)),
            pl.BlockSpec((32, STEP // 128, 16, 128), lambda i: (0, i, 0, 0)),
        ],
        out_specs=pl.BlockSpec((STEP, K), lambda i: (i, 0)),
        compiler_params=pltpu.CompilerParams(vmem_limit_bytes=VMEM),
        cost_estimate=pl.CostEstimate(
            flops=6 * 2 * K**3, bytes_accessed=6 << 20, transcendentals=0
        ),
    )(at, vh, vl, d)


def exchange(blocks, axis, n):
    blocks = blocks.reshape(n, -1, 128)
    return lax.all_to_all(blocks, axis, 0, 0).reshape(-1, 128)


def on_device(pivots, demand, prices):
    z, core, y, x = (lax.axis_index(name) for name in ("z", "core", "y", "x"))
    at = jnp.stack([z, core, y, x, pivots[0], pivots[1]]).astype(jnp.int32)
    prices_all = lax.all_gather(prices, ROW, axis=0, tiled=True)
    price_cut, demand_cut, *_ = small(
        cut_kernel, ((NX * PART, 128), (64, 128), (128, 128), (64, 128)), at, prices, demand.T
    )
    twin = lax.ppermute(demand_cut, "core", flip(NCORE, 1))
    price_cut = exchange(price_cut, "x", NX)
    price_cut, demand_cut, demand_part = small(
        sift_kernel, ((32, 128), (NZ * 32, 128), (512, 128)), at, price_cut, demand_cut, twin
    )
    demand_all = lax.all_gather(demand_part, "y", axis=0, tiled=True)
    (both,) = small(
        pick_z_kernel, ((NY * 64, 128),), at, price_cut, exchange(demand_cut, "z", NZ)
    )
    price_cut, demand_cut = small(
        pick_y_kernel, ((NZ * 32, 128), (NY * 32, 128)), at, exchange(both, "y", NY)
    )
    (packed,) = small(
        join_kernel, ((NX * 512, 128),), at, exchange(price_cut, "z", NZ), demand_cut
    )
    packed = exchange(packed, "x", NX)
    vh, vl = invert(at, packed, lax.ppermute(packed, "core", flip(NCORE, 1)), pltpu.with_memory_space_constraint(prices_all, pltpu.HBM))
    return tile(at, vh, vl, pltpu.with_memory_space_constraint(demand_all.reshape(NY * NX, 8, 16, 128), pltpu.HBM))


def solution(mesh):
    inner = Mesh(mesh.devices.reshape(NZ, NCORE, NY, NX), ROW + COL)
    placed = (P(), P(ROW, COL), P(ROW, COL))
    return jax.shard_map(
        on_device, mesh=inner, in_specs=placed, out_specs=P(ROW, COL), check_vma=False
    )
```

```python
import jax
import jax.numpy as jnp
from jax import lax
from jax.experimental import pallas as pl
from jax.experimental.pallas import tpu as pltpu
from jax.sharding import Mesh
from jax.sharding import PartitionSpec as P

PW = 256
K = 512
FAST, GAIN = 4, 1.85
VMEM = 20 << 20
NZ, NCORE, NY, NX = 8, 2, 8, 4
ROW = ("z", "core")
COL = ("y", "x")


def flip(n, bit):
    return [(i, i ^ bit) for i in range(n)]


def split(a):
    high = a.astype(jnp.bfloat16)
    return high, (a - high.astype(jnp.float32)).astype(jnp.bfloat16)


def dot1(a, b):
    return jnp.dot(a, b, preferred_element_type=jnp.float32)


def dot1_t(a, b):
    return lax.dot_general(
        a, b, (((1,), (1,)), ((), ())), preferred_element_type=jnp.float32
    )


def dot3(a, b, dot=dot1):
    return dot(a[0], b[0]) + (dot(a[0], b[1]) + dot(a[1], b[0]))


def eye(rows, cols):
    r = lax.broadcasted_iota(jnp.int32, (rows, cols), 0)
    c = lax.broadcasted_iota(jnp.int32, (rows, cols), 1)
    return (r == c).astype(jnp.float32)


PART = 160


def cut_kernel(at, p_ref, d_ref, px_ref, dp_ref, pp_ref, dd_ref):
    for q in range(4):
        pivot = at[4 + q // 2]
        start = pl.multiple_of((pivot & 1) * PW + (q % 2) * 128, 128)
        pp_ref[pl.ds(q, 32, stride=4), :] = p_ref[:, pl.ds(start, 128)]
        start = pl.multiple_of((pivot & 3) * PW + (q % 2) * 128, 128)
        dd_ref[pl.ds(q, 16, stride=4), :] = d_ref[:, pl.ds(start, 128)]
    for i in range(16):
        dp_ref[pl.ds(4 * (8 * (i % 2) + i // 2), 4), :] = dd_ref[pl.ds(4 * i, 4), :]
    for k in range(NX):
        for y in range(NY):
            px_ref[pl.ds(k * PART + 4 * y, 4), :] = pp_ref[pl.ds(4 * (4 * y + k), 4), :]
        for t in range(8):
            px_ref[pl.ds(k * PART + 32 + 16 * t, 16), :] = d_ref[:, 128 * t : 128 * t + 128]


def sift_kernel(at, px_ref, dp_ref, twin_ref, py_ref, dz_ref, d_ref):
    row = lax.broadcasted_iota(jnp.int32, (32, 128), 0) & 3
    core = at[1]
    price, mine = [], []
    for which in range(2):
        pivot = at[4 + which]
        start = pl.multiple_of(((pivot // 2) & 3) * PART, 8)
        price.append(px_ref[pl.ds(start, 32), :])
        mine.append(((pivot // 4) & 1) == core)
    py_ref[...] = jnp.where(row < 2, price[0], price[1])
    half = pl.ds(pl.multiple_of(core * 32, 32), 32)
    own, twin = dp_ref[half, :], twin_ref[half, :]
    kept = jnp.where(
        row < 2, jnp.where(mine[0], own, twin), jnp.where(mine[1], own, twin)
    )
    for k in range(NZ):
        dz_ref[pl.ds(32 * k, 32), :] = kept
    for k in range(NX):
        d_ref[pl.ds(128 * k, 128), :] = px_ref[pl.ds(k * PART + 32, 128), :]


def pick_z_kernel(at, py_ref, dz_ref, o_ref):
    row = lax.broadcasted_iota(jnp.int32, (32, 128), 0) & 3
    parts = [dz_ref[pl.ds(pl.multiple_of((at[4 + w] // 8) * 32, 32), 32), :] for w in range(2)]
    kept = jnp.where(row < 2, parts[0], parts[1])
    for k in range(NY):
        o_ref[pl.ds(64 * k, 32), :] = py_ref[...]
        o_ref[pl.ds(64 * k + 32, 32), :] = kept


def pick_y_kernel(at, y_ref, pz_ref, dx_ref):
    row = lax.broadcasted_iota(jnp.int32, (32, 128), 0) & 3
    parts = [y_ref[pl.ds(pl.multiple_of((at[4 + w] // 8) * 64, 64), 32), :] for w in range(2)]
    kept = jnp.where(row < 2, parts[0], parts[1])
    for k in range(NZ):
        pz_ref[pl.ds(32 * k, 32), :] = kept
    for k in range(NY):
        dx_ref[pl.ds(32 * k, 32), :] = y_ref[pl.ds(64 * k + 32, 32), :]


def join_kernel(at, pz_ref, dx_ref, o_ref):
    for k in range(NX):
        o_ref[pl.ds(512 * k, 256), :] = pz_ref[...]
        o_ref[pl.ds(512 * k + 256, 256), :] = dx_ref[...]


def small(kernel, shapes, at, *parts):
    return pl.pallas_call(
        kernel,
        out_shape=[jax.ShapeDtypeStruct(shape, jnp.float32) for shape in shapes],
        in_specs=[pl.BlockSpec(memory_space=pltpu.SMEM)]
        + [pl.BlockSpec(memory_space=pltpu.VMEM)] * len(parts),
        out_specs=[pl.BlockSpec(memory_space=pltpu.VMEM)] * len(shapes),
        compiler_params=pltpu.CompilerParams(vmem_limit_bytes=VMEM),
    )(at, *parts)


def slab_row(n, of_prices):
    core, x, high, low = n >> 8, (n >> 6) & 3, (n >> 3) & 7, n & 7
    if of_prices:
        return 64 * high + 32 * core + 4 * low + x
    return 64 * high + 16 * x + 2 * low + core


def invert_kernel(
    at, own, other, slab, vh_ref, vl_ref, x_ref, b_ref, bh_ref, bl_ref, pj_ref, dj_ref,
    slab_ref, sem,
):
    core, y, x, first, second = (at[i] for i in range(1, 6))
    fetch = pltpu.make_async_copy(slab, slab_ref, sem)
    fetch.start()
    for ref, side in ((own, core), (other, 1 - core)):
        for k in range(NX):
            to = pl.ds(pl.multiple_of(side * 256 + 64 * k, 64), 64)
            for q in range(4):
                lanes = slice(128 * q, 128 * q + 128)
                pj_ref[to, lanes] = ref[pl.ds(512 * k + q, 64, stride=4), :]
                dj_ref[to, lanes] = ref[pl.ds(512 * k + 256 + q, 64, stride=4), :]
    n0 = lax.broadcasted_iota(jnp.int32, (K, 128), 0)
    n1 = lax.broadcasted_iota(jnp.int32, (8, K), 1)

    def match(down, across):
        down, across = jnp.concatenate([down] * 4, 1), jnp.concatenate([across] * 64, 0)
        return (down == across).astype(jnp.float32)

    b = match(slab_row(n0, True), slab_row(n1, False)) - dot3(split(pj_ref[...]), split(dj_ref[...]), dot1_t)
    b_ref[...] = b
    size = jnp.max(jnp.sum(jnp.abs(b), axis=0)) * jnp.max(jnp.sum(jnp.abs(b), axis=1))
    bh, bl = split(b)
    bh_ref[...] = bh
    bl_ref[...] = bl
    x_ref[...] = b.T / size

    def coarse_step(gain, measured):
        xv = x_ref[...]
        xh = xv.astype(jnp.bfloat16)
        r = eye(K, K) - dot1(bh_ref[...], xh)
        xv = xv + dot1(xh, r.astype(jnp.bfloat16))
        x_ref[...] = xv * gain if gain != 1.0 else xv
        return jnp.sum(r * r) if measured else None

    for _ in range(FAST):
        coarse_step(GAIN, False)

    def coarse(carry):
        coarse_step(1.0, False)
        return carry[0] + 1, coarse_step(1.0, True)

    lax.while_loop(
        lambda c: (c[0] < 20) & (c[1] > 0.3) & (c[1] < 4.0 * K),
        coarse,
        (jnp.int32(0), jnp.float32(K)),
    )

    def fine(carry):
        count, last, _ = carry
        xv = x_ref[...]
        xs = split(xv)
        r = eye(K, K) - dot3((bh_ref[...], bl_ref[...]), xs)
        now = jnp.sum(r * r)
        lost = (count == 0) & jnp.logical_not(now < K)
        x_ref[...] = xv + dot1(xs[0], r.astype(jnp.bfloat16))

        @pl.when(lost)
        def _():
            x_ref[...] = b_ref[...].T / size

        stuck = (now > 0.25 * last) & (now < 0.1)
        return count + 1, now, lost | ((now > 1e-5) & jnp.logical_not(stuck))

    lax.while_loop(
        lambda c: (c[0] < 60) & c[2],
        fine,
        (jnp.int32(0), jnp.float32(8.0 * K), jnp.bool_(True)),
    )

    spread = jnp.sum(b_ref[...] * b_ref[...]) * jnp.sum(x_ref[...] * x_ref[...])

    @pl.when(spread > 2e6)
    def _():
        xv = x_ref[...]
        r = eye(K, K) - jnp.dot(
            b_ref[...], xv, precision=lax.Precision.HIGHEST, preferred_element_type=jnp.float32
        )
        x_ref[...] = xv + dot3(split(xv), split(r))

    order = match(slab_row(n0, True), n1).astype(jnp.bfloat16)
    fetch.wait()
    sh, sl = split(slab_ref[...])
    rows = dot1(order, sh).astype(jnp.bfloat16), dot1(order, sl).astype(jnp.bfloat16)
    v = dot3(split(x_ref[...]), rows)
    col = lax.broadcasted_iota(jnp.int32, (1, K), 1) + (y * NX + x) * K
    gone = (col // PW == first) | (col // PW == second)
    vh, vl = split(jnp.where(gone, 0.0, v))
    order = match(n0, slab_row(n1, False)).astype(jnp.bfloat16)
    vh_ref[...] = dot1(order, vh).astype(jnp.bfloat16)
    vl_ref[...] = dot1(order, vl).astype(jnp.bfloat16)


def invert(at, own, other, slab):
    f32, bf16 = jnp.float32, jnp.bfloat16
    return pl.pallas_call(
        invert_kernel,
        out_shape=[jax.ShapeDtypeStruct((K, K), bf16)] * 2,
        in_specs=[pl.BlockSpec(memory_space=pltpu.SMEM)]
        + [pl.BlockSpec(memory_space=pltpu.VMEM)] * 2
        + [pl.BlockSpec(memory_space=pltpu.HBM)],
        out_specs=[pl.BlockSpec(memory_space=pltpu.VMEM)] * 2,
        scratch_shapes=[pltpu.VMEM((K, K), f32)] * 2
        + [pltpu.VMEM((K, K), bf16)] * 2
        + [pltpu.VMEM((K, K), f32)] * 3
        + [pltpu.SemaphoreType.DMA],
        compiler_params=pltpu.CompilerParams(vmem_limit_bytes=VMEM),
        cost_estimate=pl.CostEstimate(
            flops=60 * 2 * K**3, bytes_accessed=5 << 20, transcendentals=0
        ),
    )(at, own, other, slab)


STEP = 512


def tile_kernel(at, vh_ref, vl_ref, d_ref, o_ref):
    z, core, y, x, first, second = (at[i] for i in range(6))
    base = (z * NCORE + core) * 1024 + pl.program_id(0) * STEP
    d = split(
        jnp.concatenate([d_ref[:, t].reshape(K, 128).T for t in range(STEP // 128)], 0)
    )
    row = lax.broadcasted_iota(jnp.int32, (STEP, 1), 0) + base
    col = lax.broadcasted_iota(jnp.int32, (1, K), 1) + (y * NX + x) * K
    kept = (row // PW != first) & (row // PW != second)
    gone = (col // PW == first) | (col // PW == second)
    tile = ((row == col) & jnp.logical_not(gone)).astype(jnp.float32)
    tile = tile - dot3(d, (vh_ref[...], vl_ref[...]))
    o_ref[...] = jnp.where(kept, tile, 0.0)


def tile(at, vh, vl, d):
    rows = 128 * d.shape[1]
    return pl.pallas_call(
        tile_kernel,
        grid=(rows // STEP,),
        out_shape=jax.ShapeDtypeStruct((rows, K), jnp.float32),
        in_specs=[
            pl.BlockSpec(memory_space=pltpu.SMEM),
            pl.BlockSpec((K, K), lambda i: (0, 0)),
            pl.BlockSpec((K, K), lambda i: (0, 0)),
            pl.BlockSpec((32, STEP // 128, 16, 128), lambda i: (0, i, 0, 0)),
        ],
        out_specs=pl.BlockSpec((STEP, K), lambda i: (i, 0)),
        compiler_params=pltpu.CompilerParams(vmem_limit_bytes=VMEM),
        cost_estimate=pl.CostEstimate(
            flops=6 * 2 * K**3, bytes_accessed=6 << 20, transcendentals=0
        ),
    )(at, vh, vl, d)


def exchange(blocks, axis, n):
    blocks = blocks.reshape(n, -1, 128)
    return lax.all_to_all(blocks, axis, 0, 0).reshape(-1, 128)


def on_device(pivots, demand, prices):
    z, core, y, x = (lax.axis_index(name) for name in ("z", "core", "y", "x"))
    at = jnp.stack([z, core, y, x, pivots[0], pivots[1]]).astype(jnp.int32)
    prices_all = lax.all_gather(prices, ROW, axis=0, tiled=True)
    price_cut, demand_cut, *_ = small(
        cut_kernel, ((NX * PART, 128), (64, 128), (128, 128), (64, 128)), at,
        pltpu.with_memory_space_constraint(prices, pltpu.HBM),
        pltpu.with_memory_space_constraint(demand.T, pltpu.HBM),
    )
    twin = lax.ppermute(demand_cut, "core", flip(NCORE, 1))
    price_cut = exchange(price_cut, "x", NX)
    price_cut, demand_cut, demand_part = small(
        sift_kernel, ((32, 128), (NZ * 32, 128), (512, 128)), at, price_cut, demand_cut, twin
    )
    demand_all = lax.all_gather(demand_part, "y", axis=0, tiled=True)
    (both,) = small(
        pick_z_kernel, ((NY * 64, 128),), at, price_cut, exchange(demand_cut, "z", NZ)
    )
    price_cut, demand_cut = small(
        pick_y_kernel, ((NZ * 32, 128), (NY * 32, 128)), at, exchange(both, "y", NY)
    )
    (packed,) = small(
        join_kernel, ((NX * 512, 128),), at, exchange(price_cut, "z", NZ), demand_cut
    )
    packed = exchange(packed, "x", NX)
    vh, vl = invert(at, packed, lax.ppermute(packed, "core", flip(NCORE, 1)), pltpu.with_memory_space_constraint(prices_all, pltpu.HBM))
    return tile(at, vh, vl, pltpu.with_memory_space_constraint(demand_all.reshape(NY * NX, 8, 16, 128), pltpu.HBM))


def solution(mesh):
    inner = Mesh(mesh.devices.reshape(NZ, NCORE, NY, NX), ROW + COL)
    placed = (P(), P(ROW, COL), P(ROW, COL))
    return jax.shard_map(
        on_device, mesh=inner, in_specs=placed, out_specs=P(ROW, COL), check_vma=False
    )
```

```python
import jax
import jax.numpy as jnp
from jax import lax
from jax.experimental import pallas as pl
from jax.experimental.pallas import tpu as pltpu
from jax.sharding import Mesh
from jax.sharding import PartitionSpec as P

PW = 256
K = 512
FAST, GAIN = 4, 1.85
VMEM = 20 << 20
NZ, NCORE, NY, NX = 8, 2, 8, 4
ROW = ("z", "core")
COL = ("y", "x")


def flip(n, bit):
    return [(i, i ^ bit) for i in range(n)]


def split(a):
    high = a.astype(jnp.bfloat16)
    return high, (a - high.astype(jnp.float32)).astype(jnp.bfloat16)


def dot1(a, b):
    return jnp.dot(a, b, preferred_element_type=jnp.float32)


def dot1_t(a, b):
    return lax.dot_general(
        a, b, (((1,), (1,)), ((), ())), preferred_element_type=jnp.float32
    )


def dot3(a, b, dot=dot1):
    return dot(a[0], b[0]) + (dot(a[0], b[1]) + dot(a[1], b[0]))


def eye(rows, cols):
    r = lax.broadcasted_iota(jnp.int32, (rows, cols), 0)
    c = lax.broadcasted_iota(jnp.int32, (rows, cols), 1)
    return (r == c).astype(jnp.float32)


PART = 160


def cut_kernel(at, p_ref, d_ref, px_ref, dp_ref, pp_ref, dd_ref):
    for q in range(4):
        pivot = at[4 + q // 2]
        start = pl.multiple_of((pivot & 1) * PW + (q % 2) * 128, 128)
        pp_ref[pl.ds(q, 32, stride=4), :] = p_ref[:, pl.ds(start, 128)]
        start = pl.multiple_of((pivot & 3) * PW + (q % 2) * 128, 128)
        dd_ref[pl.ds(q, 16, stride=4), :] = d_ref[:, pl.ds(start, 128)]
    for i in range(16):
        dp_ref[pl.ds(4 * (8 * (i % 2) + i // 2), 4), :] = dd_ref[pl.ds(4 * i, 4), :]
    for k in range(NX):
        for y in range(NY):
            px_ref[pl.ds(k * PART + 4 * y, 4), :] = pp_ref[pl.ds(4 * (4 * y + k), 4), :]
        for t in range(8):
            px_ref[pl.ds(k * PART + 32 + 16 * t, 16), :] = d_ref[:, 128 * t : 128 * t + 128]


def sift_kernel(at, px_ref, dp_ref, twin_ref, py_ref, dz_ref, d_ref):
    row = lax.broadcasted_iota(jnp.int32, (32, 128), 0) & 3
    core = at[1]
    price, mine = [], []
    for which in range(2):
        pivot = at[4 + which]
        start = pl.multiple_of(((pivot // 2) & 3) * PART, 8)
        price.append(px_ref[pl.ds(start, 32), :])
        mine.append(((pivot // 4) & 1) == core)
    py_ref[...] = jnp.where(row < 2, price[0], price[1])
    half = pl.ds(pl.multiple_of(core * 32, 32), 32)
    own, twin = dp_ref[half, :], twin_ref[half, :]
    kept = jnp.where(
        row < 2, jnp.where(mine[0], own, twin), jnp.where(mine[1], own, twin)
    )
    for k in range(NZ):
        dz_ref[pl.ds(32 * k, 32), :] = kept
    for k in range(NX):
        d_ref[pl.ds(128 * k, 128), :] = px_ref[pl.ds(k * PART + 32, 128), :]


def pick_z_kernel(at, py_ref, dz_ref, o_ref):
    row = lax.broadcasted_iota(jnp.int32, (32, 128), 0) & 3
    parts = [dz_ref[pl.ds(pl.multiple_of((at[4 + w] // 8) * 32, 32), 32), :] for w in range(2)]
    kept = jnp.where(row < 2, parts[0], parts[1])
    for k in range(NY):
        o_ref[pl.ds(64 * k, 32), :] = py_ref[...]
        o_ref[pl.ds(64 * k + 32, 32), :] = kept


def pick_y_kernel(at, y_ref, pz_ref, dx_ref):
    row = lax.broadcasted_iota(jnp.int32, (32, 128), 0) & 3
    parts = [y_ref[pl.ds(pl.multiple_of((at[4 + w] // 8) * 64, 64), 32), :] for w in range(2)]
    kept = jnp.where(row < 2, parts[0], parts[1])
    for k in range(NZ):
        pz_ref[pl.ds(32 * k, 32), :] = kept
    for k in range(NY):
        dx_ref[pl.ds(32 * k, 32), :] = y_ref[pl.ds(64 * k + 32, 32), :]


def join_kernel(at, pz_ref, dx_ref, o_ref):
    for k in range(NX):
        o_ref[pl.ds(512 * k, 256), :] = pz_ref[...]
        o_ref[pl.ds(512 * k + 256, 256), :] = dx_ref[...]


def small(kernel, shapes, at, *parts):
    return pl.pallas_call(
        kernel,
        out_shape=[jax.ShapeDtypeStruct(shape, jnp.float32) for shape in shapes],
        in_specs=[pl.BlockSpec(memory_space=pltpu.SMEM)]
        + [pl.BlockSpec(memory_space=pltpu.VMEM)] * len(parts),
        out_specs=[pl.BlockSpec(memory_space=pltpu.VMEM)] * len(shapes),
        compiler_params=pltpu.CompilerParams(vmem_limit_bytes=VMEM),
    )(at, *parts)


def slab_row(n, of_prices):
    core, x, high, low = n >> 8, (n >> 6) & 3, (n >> 3) & 7, n & 7
    if of_prices:
        return 64 * high + 32 * core + 4 * low + x
    return 64 * high + 16 * x + 2 * low + core


def invert_kernel(
    at, own, other, slab, vh_ref, vl_ref, x_ref, b_ref, bh_ref, bl_ref, pj_ref, dj_ref,
    slab_ref, sem,
):
    core, y, x, first, second = (at[i] for i in range(1, 6))
    fetch = pltpu.make_async_copy(slab, slab_ref, sem)
    fetch.start()
    for ref, side in ((own, core), (other, 1 - core)):
        for k in range(NX):
            to = pl.ds(pl.multiple_of(side * 256 + 64 * k, 64), 64)
            for q in range(4):
                lanes = slice(128 * q, 128 * q + 128)
                pj_ref[to, lanes] = ref[pl.ds(512 * k + q, 64, stride=4), :]
                dj_ref[to, lanes] = ref[pl.ds(512 * k + 256 + q, 64, stride=4), :]
    n0 = lax.broadcasted_iota(jnp.int32, (K, 128), 0)
    n1 = lax.broadcasted_iota(jnp.int32, (8, K), 1)

    def match(down, across):
        down, across = jnp.concatenate([down] * 4, 1), jnp.concatenate([across] * 64, 0)
        return (down == across).astype(jnp.float32)

    b = match(slab_row(n0, True), slab_row(n1, False)) - dot3(split(pj_ref[...]), split(dj_ref[...]), dot1_t)
    b_ref[...] = b
    size = jnp.max(jnp.sum(jnp.abs(b), axis=0)) * jnp.max(jnp.sum(jnp.abs(b), axis=1))
    bh, bl = split(b)
    bh_ref[...] = bh
    bl_ref[...] = bl
    x_ref[...] = b.T / size

    def coarse_step(gain, measured):
        xv = x_ref[...]
        xh = xv.astype(jnp.bfloat16)
        r = eye(K, K) - dot1(bh_ref[...], xh)
        xv = xv + dot1(xh, r.astype(jnp.bfloat16))
        x_ref[...] = xv * gain if gain != 1.0 else xv
        return jnp.sum(r * r) if measured else None

    for _ in range(FAST):
        coarse_step(GAIN, False)

    def coarse(carry):
        coarse_step(1.0, False)
        return carry[0] + 1, coarse_step(1.0, True)

    lax.while_loop(
        lambda c: (c[0] < 20) & (c[1] > 0.3) & (c[1] < 4.0 * K),
        coarse,
        (jnp.int32(0), jnp.float32(K)),
    )

    def fine(carry):
        count, last, _ = carry
        xv = x_ref[...]
        xs = split(xv)
        r = eye(K, K) - dot3((bh_ref[...], bl_ref[...]), xs)
        now = jnp.sum(r * r)
        lost = (count == 0) & jnp.logical_not(now < K)
        x_ref[...] = xv + dot1(xs[0], r.astype(jnp.bfloat16))

        @pl.when(lost)
        def _():
            x_ref[...] = b_ref[...].T / size

        stuck = (now > 0.25 * last) & (now < 0.1)
        return count + 1, now, lost | ((now > 1e-5) & jnp.logical_not(stuck))

    lax.while_loop(
        lambda c: (c[0] < 60) & c[2],
        fine,
        (jnp.int32(0), jnp.float32(8.0 * K), jnp.bool_(True)),
    )

    spread = jnp.sum(b_ref[...] * b_ref[...]) * jnp.sum(x_ref[...] * x_ref[...])

    @pl.when(spread > 2e6)
    def _():
        xv = x_ref[...]
        r = eye(K, K) - jnp.dot(
            b_ref[...], xv, precision=lax.Precision.HIGHEST, preferred_element_type=jnp.float32
        )
        x_ref[...] = xv + dot3(split(xv), split(r))

    order = match(slab_row(n0, True), n1).astype(jnp.bfloat16)
    fetch.wait()
    sh, sl = split(slab_ref[...])
    rows = dot1(order, sh).astype(jnp.bfloat16), dot1(order, sl).astype(jnp.bfloat16)
    v = dot3(split(x_ref[...]), rows)
    col = lax.broadcasted_iota(jnp.int32, (1, K), 1) + (y * NX + x) * K
    gone = (col // PW == first) | (col // PW == second)
    vh, vl = split(jnp.where(gone, 0.0, v))
    order = match(n0, slab_row(n1, False)).astype(jnp.bfloat16)
    vh_ref[...] = dot1(order, vh).astype(jnp.bfloat16)
    vl_ref[...] = dot1(order, vl).astype(jnp.bfloat16)


def invert(at, own, other, slab):
    f32, bf16 = jnp.float32, jnp.bfloat16
    return pl.pallas_call(
        invert_kernel,
        out_shape=[jax.ShapeDtypeStruct((K, K), bf16)] * 2,
        in_specs=[pl.BlockSpec(memory_space=pltpu.SMEM)]
        + [pl.BlockSpec(memory_space=pltpu.VMEM)] * 2
        + [pl.BlockSpec(memory_space=pltpu.HBM)],
        out_specs=[pl.BlockSpec(memory_space=pltpu.VMEM)] * 2,
        scratch_shapes=[pltpu.VMEM((K, K), f32)] * 2
        + [pltpu.VMEM((K, K), bf16)] * 2
        + [pltpu.VMEM((K, K), f32)] * 3
        + [pltpu.SemaphoreType.DMA],
        compiler_params=pltpu.CompilerParams(vmem_limit_bytes=VMEM),
        cost_estimate=pl.CostEstimate(
            flops=60 * 2 * K**3, bytes_accessed=5 << 20, transcendentals=0
        ),
    )(at, own, other, slab)


STEP = 512


def tile_kernel(at, vh_ref, vl_ref, d_ref, o_ref):
    z, core, y, x, first, second = (at[i] for i in range(6))
    base = (z * NCORE + core) * 1024 + pl.program_id(0) * STEP
    d = split(
        jnp.concatenate([d_ref[:, t].reshape(K, 128).T for t in range(STEP // 128)], 0)
    )
    row = lax.broadcasted_iota(jnp.int32, (STEP, 1), 0) + base
    col = lax.broadcasted_iota(jnp.int32, (1, K), 1) + (y * NX + x) * K
    kept = (row // PW != first) & (row // PW != second)
    gone = (col // PW == first) | (col // PW == second)
    tile = ((row == col) & jnp.logical_not(gone)).astype(jnp.float32)
    tile = tile - dot3(d, (vh_ref[...], vl_ref[...]))
    o_ref[...] = jnp.where(kept, tile, 0.0)


def tile(at, vh, vl, d):
    rows = 128 * d.shape[1]
    return pl.pallas_call(
        tile_kernel,
        grid=(rows // STEP,),
        out_shape=jax.ShapeDtypeStruct((rows, K), jnp.float32),
        in_specs=[
            pl.BlockSpec(memory_space=pltpu.SMEM),
            pl.BlockSpec((K, K), lambda i: (0, 0)),
            pl.BlockSpec((K, K), lambda i: (0, 0)),
            pl.BlockSpec((32, STEP // 128, 16, 128), lambda i: (0, i, 0, 0)),
        ],
        out_specs=pl.BlockSpec((STEP, K), lambda i: (i, 0)),
        compiler_params=pltpu.CompilerParams(vmem_limit_bytes=VMEM),
        cost_estimate=pl.CostEstimate(
            flops=6 * 2 * K**3, bytes_accessed=6 << 20, transcendentals=0
        ),
    )(at, vh, vl, d)


def exchange(blocks, axis, n):
    blocks = blocks.reshape(n, -1, 128)
    return lax.all_to_all(blocks, axis, 0, 0).reshape(-1, 128)


def on_device(pivots, demand, prices):
    z, core, y, x = (lax.axis_index(name) for name in ("z", "core", "y", "x"))
    at = jnp.stack([z, core, y, x, pivots[0], pivots[1]]).astype(jnp.int32)
    prices_all = lax.all_gather(prices, ROW, axis=0, tiled=True)
    price_cut, demand_cut, *_ = small(
        cut_kernel, ((NX * PART, 128), (64, 128), (128, 128), (64, 128)), at,
        pltpu.with_memory_space_constraint(prices, pltpu.HBM),
        pltpu.with_memory_space_constraint(demand.T, pltpu.HBM),
    )
    twin = lax.ppermute(demand_cut, "core", flip(NCORE, 1))
    price_cut = exchange(price_cut, "x", NX)
    price_cut, demand_cut, demand_part = small(
        sift_kernel, ((32, 128), (NZ * 32, 128), (512, 128)), at, price_cut, demand_cut, twin
    )
    (both,) = small(
        pick_z_kernel, ((NY * 64, 128),), at, price_cut, exchange(demand_cut, "z", NZ)
    )
    price_cut, demand_cut = small(
        pick_y_kernel, ((NZ * 32, 128), (NY * 32, 128)), at, exchange(both, "y", NY)
    )
    demand_part, price_cut = lax.optimization_barrier((demand_part, price_cut))
    demand_all = lax.all_gather(demand_part, "y", axis=0, tiled=True)
    (packed,) = small(
        join_kernel, ((NX * 512, 128),), at, exchange(price_cut, "z", NZ), demand_cut
    )
    packed = exchange(packed, "x", NX)
    vh, vl = invert(at, packed, lax.ppermute(packed, "core", flip(NCORE, 1)), pltpu.with_memory_space_constraint(prices_all, pltpu.HBM))
    return tile(at, vh, vl, pltpu.with_memory_space_constraint(demand_all.reshape(NY * NX, 8, 16, 128), pltpu.HBM))


def solution(mesh):
    inner = Mesh(mesh.devices.reshape(NZ, NCORE, NY, NX), ROW + COL)
    placed = (P(), P(ROW, COL), P(ROW, COL))
    return jax.shard_map(
        on_device, mesh=inner, in_specs=placed, out_specs=P(ROW, COL), check_vma=False
    )
```
